128 devices in a mesh: oct: 2 (over core), sub: 64 (over x, z, y).
Axes of the slice: x: 4, y: 4, z: 4, core: 2. Of those that a mesh axis runs over, the one named last changes fastest.
Arguments:
- coefficients: float32 [2048, 4096], P(('oct', 'sub')), may hold values from -6 to 6
- potential: float32 [2048, 4096], P(('oct', 'sub')), may hold values from 0.2 to 2
- to_values: float32 [16, 16], replicated, may hold values from -1.5 to 1.5
- x_kernels: bfloat16 [20, 48, 16], replicated, may hold values from -0.5 to 0.5
- yz_kernels: bfloat16 [256, 46080], replicated, may hold values from -0.046875 to 0.046875
- two_scale: float32 [2, 16, 16], replicated, may hold values from -1 to 1
- disp_ids: int32 [2048, 16], P(('oct', 'sub')), may hold values from -1 to 26, as said below
- dest_box: int32 [2048, 16], P(('oct', 'sub')), may hold values from -1 to 2047, as said below
- parent_of: int32 [2048], P(('oct', 'sub')), may hold values from 0 to 255, as said below
- child_octant: int32 [2048], P(('oct', 'sub')), may hold values from 0 to 7
Outputs:
- next_field: float32 [2048, 4096], P(('oct', 'sub'))
- parents: float32 [256, 4096], P(('oct', 'sub'))
The draws below stay inside these ranges and needn't reach their ends.
Inputs may be any that keep to these rules, and one draw needn't show every extreme that they name: `disp_ids`: -1 marks an empty slot, exactly where dest_box is -1; in every row the live slots come first, 4 or more of them. `dest_box`: among the live slots of one aligned block of 16 rows, at most 2 name boxes of any one aligned block of 16 boxes; some box block receives exactly 2 from every row block. Every parent is named by exactly 8 boxes, whose child_octant values are 0 to 7; parent_of[b] // 128 == b // 1024. Within one aligned block of 16 boxes, at most 1 box has its parent in any one aligned block of 2 parents, and some parent block is named by exactly 1 of them.
All inputs are finite; a program needn't handle non-finite values.
Results may differ from the reference program's by a relative error of at most 0.018.
Values may be sent and summed in bfloat16 or wider, within the bound.
A program may use at most 192 MiB of HBM per device.

```python
import math
import jax
import jax.numpy as jnp
from jax import lax

K = 16
TERMS = 20
LIST = 16
ITERS = 2
BOX_DEV = 16
BOXES = 2048
GROUP_BOXES = 1024
PARENTS = 256
CAP = 2
N_OCT = 2
N_SUB = 64


def route_tables(key):
    base = jax.random.fold_in(key, 7)
    key_len, key_perm, key_pick, key_disp, key_local = jax.random.split(base, 5)
    devices_all = N_OCT * N_SUB
    lengths = jax.random.randint(key_len, (devices_all, BOX_DEV, 1), LIST // 4, LIST + 1)
    slot_ids = jnp.arange(LIST, dtype=jnp.int32)
    is_live = slot_ids[None, None, :] < lengths
    position = slot_ids[None, :] * BOX_DEV + jnp.arange(BOX_DEV, dtype=jnp.int32)[:, None]
    group_ids = position // CAP
    target = jax.random.randint(key_pick, (), 0, devices_all)
    orderings = jax.vmap(lambda single: jax.random.permutation(single, devices_all))(jax.random.split(key_perm, devices_all))
    leading = orderings[:, :1]
    orderings = jnp.where(orderings == target, leading, orderings)
    orderings = orderings.at[:, 0].set(target)
    owners = orderings[:, group_ids]
    local_ids = jax.random.randint(key_local, (devices_all, BOX_DEV, LIST), 0, BOX_DEV)
    dest_ids = jnp.where(is_live, owners * BOX_DEV + local_ids, -1)
    disp_vals = jnp.where(is_live, jax.random.randint(key_disp, (devices_all, BOX_DEV, LIST), 0, 27), -1)
    return (disp_vals.reshape(BOXES, LIST).astype(jnp.int32), dest_ids.reshape(BOXES, LIST).astype(jnp.int32))


def group_tree(key_shift, key_rank, key_place):
    parent_local = BOX_DEV // 8
    slots = jnp.arange(BOX_DEV, dtype=jnp.int32)
    shift_ids = jnp.arange(N_SUB, dtype=jnp.int32)
    scores = jax.random.permutation(key_shift, N_SUB).astype(jnp.int32)
    forced = (shift_ids == 1) | (shift_ids == N_SUB - 1) | (shift_ids == N_SUB // 2)
    scores = jnp.where(forced, scores - N_SUB, scores)
    shift_order = jnp.argsort(scores, stable=True).astype(jnp.int32)
    shifts = shift_order[slots % N_SUB]
    senders = jnp.arange(N_SUB, dtype=jnp.int32)[:, None]
    owners = (senders + shifts[None, :]) % N_SUB
    ranks = jax.vmap(lambda single: jax.random.permutation(single, BOX_DEV))(jax.random.split(key_rank, N_SUB)).astype(jnp.int32)
    rank_at = ranks[owners, slots[None, :]]
    parent_vals = owners * parent_local + rank_at // 8
    octant_vals = rank_at % 8
    places = jax.vmap(lambda single: jax.random.permutation(single, BOX_DEV))(jax.random.split(key_place, N_SUB)).astype(jnp.int32)
    blank = jnp.zeros((N_SUB, BOX_DEV), jnp.int32)
    parent_rows = blank.at[senders, places].set(parent_vals)
    octant_rows = blank.at[senders, places].set(octant_vals)
    return (parent_rows.reshape(GROUP_BOXES), octant_rows.reshape(GROUP_BOXES))


def tree_tables(key):
    base = jax.random.fold_in(key, 11)
    key_shift, key_rank, key_place = jax.random.split(base, 3)
    parent_rows, octant_rows = jax.vmap(group_tree)(jax.random.split(key_shift, N_OCT), jax.random.split(key_rank, N_OCT), jax.random.split(key_place, N_OCT))
    offsets = jnp.arange(N_OCT, dtype=jnp.int32)[:, None] * (GROUP_BOXES // 8)
    parent_rows = parent_rows + offsets
    return (parent_rows.reshape(BOXES).astype(jnp.int32), octant_rows.reshape(BOXES).astype(jnp.int32))


def draw_disp_ids(key, part):
    return route_tables(key)[0]


def draw_dest_box(key, part):
    return route_tables(key)[1]


def draw_parent_of(key, part):
    return tree_tables(key)[0]


def draw_child_octant(key, part):
    return tree_tables(key)[1]


def levels(stream_key, extent, cuts, least, top_value):
    gain = 1.0
    for dim, parts in cuts:
        heights = jax.random.uniform(jax.random.fold_in(jax.random.fold_in(stream_key, 6), dim), (parts,), jnp.float32, least / len(cuts), top_value / len(cuts))
        gain = gain * jnp.repeat(jnp.exp(heights), extent[dim] // parts).reshape((-1,) + (1,) * (len(extent) - 1 - dim))
    return gain


def bell_draw(stream_key, extent, deviation, reach, cuts=(), kind=jnp.bfloat16):
    values = deviation * jax.random.normal(stream_key, extent, jnp.float32)
    if cuts:
        values = values * levels(stream_key, extent, cuts, -0.22, 0.18)
    return jnp.clip(values, -reach, reach).astype(kind)


def setup_inputs(seed: int = 0) -> dict:
    seeds = jax.random.split(jax.random.key(seed), 11)
    return {
        "coefficients": bell_draw(seeds[0], (BOXES, K**3), 1.0, 6.0, ((0, 128),), jnp.float32),
        "potential": jnp.clip(jnp.exp(math.log(2.0) - 2.3025851 * jax.random.uniform(seeds[1], (BOXES, K**3), jnp.float32) ** levels(seeds[1], (BOXES, K**3), ((0, 128),), -0.2, 0.2)), 0.2, 2.0),
        "to_values": bell_draw(seeds[2], (K, K), K ** -0.5, 1.5, (), jnp.float32),
        "x_kernels": bell_draw(seeds[3], (TERMS, 3 * K, K), (8 * K) ** -0.5, 0.5),
        "yz_kernels": bell_draw(seeds[4], (K * K, TERMS * 9 * K * K), (64 * K * K) ** -0.5, 0.046875),
        "two_scale": bell_draw(seeds[5], (2, K, K), (2 * K) ** -0.5, 1.0, (), jnp.float32),
        "disp_ids": draw_disp_ids(jax.random.fold_in(seeds[10], 71), 0),
        "dest_box": draw_dest_box(jax.random.fold_in(seeds[10], 71), 0),
        "parent_of": draw_parent_of(jax.random.fold_in(seeds[10], 71), 0),
        "child_octant": draw_child_octant(jax.random.fold_in(seeds[10], 71), 0),
    }


def transform_three(blocks, along_x, along_y, along_z):
    highest = lax.Precision.HIGHEST
    cube_view = blocks.reshape(blocks.shape[0], K, K, K)
    cube_view = jnp.einsum("ix,bxyz->biyz", along_x, cube_view, precision=highest)
    cube_view = jnp.einsum("jy,biyz->bijz", along_y, cube_view, precision=highest)
    cube_view = jnp.einsum("kz,bijz->bijk", along_z, cube_view, precision=highest)
    return cube_view.reshape(blocks.shape[0], K ** 3)


def lift_each(blocks, filters, octant):
    highest = lax.Precision.HIGHEST
    along_x = filters[octant // 4]
    along_y = filters[(octant // 2) % 2]
    along_z = filters[octant % 2]
    cube_view = blocks.reshape(blocks.shape[0], K, K, K)
    cube_view = jnp.einsum("bix,bxyz->biyz", along_x, cube_view, precision=highest)
    cube_view = jnp.einsum("bjy,biyz->bijz", along_y, cube_view, precision=highest)
    cube_view = jnp.einsum("bkz,bijz->bijk", along_z, cube_view, precision=highest)
    return cube_view.reshape(blocks.shape[0], K ** 3)


def reference(coefficients, potential, to_values, x_kernels, yz_kernels, two_scale, disp_ids, dest_box, parent_of, child_octant):
    highest = lax.Precision.HIGHEST
    plane_size = K * K
    cube_size = K ** 3
    block_boxes = 16
    count_blocks = BOXES // block_boxes
    x_wide = x_kernels.astype(jnp.float32)
    flipped = jnp.swapaxes(two_scale, 1, 2)
    current = coefficients
    parents = jnp.zeros((PARENTS, cube_size), jnp.float32)
    for iteration in range(ITERS):
        values = transform_three(current, to_values, to_values, to_values)
        product = values * (potential + 0.25 * values * values)
        source = transform_three(product, to_values.T, to_values.T, to_values.T).astype(jnp.bfloat16)

        def convolve(running, block_items):
            source_blk, disp_blk, dest_blk = block_items
            partial_value = jnp.dot(source_blk.reshape(block_boxes * K, plane_size), yz_kernels, preferred_element_type=jnp.float32).astype(jnp.bfloat16)
            partial_value = lax.optimization_barrier(partial_value).astype(jnp.float32).reshape(block_boxes, K, TERMS, 9 * plane_size)
            convolved = jnp.einsum("bxmr,max->bar", partial_value, x_wide, precision=highest)
            convolved = convolved.reshape(block_boxes, 3, K, 9, plane_size).transpose(0, 1, 3, 2, 4).reshape(block_boxes, 27, cube_size)
            picked = jnp.take_along_axis(convolved, jnp.maximum(disp_blk, 0)[:, :, None], axis=1).astype(jnp.bfloat16)
            picked = lax.optimization_barrier(picked).astype(jnp.float32)
            target = jnp.where(dest_blk < 0, BOXES, dest_blk).reshape(-1)
            running = running.at[target].add(picked.reshape(-1, cube_size), mode="drop")
            return running, None

        gathered, unused = lax.scan(
            convolve,
            jnp.zeros((BOXES, cube_size), jnp.float32),
            (source.reshape(count_blocks, block_boxes, cube_size),
             disp_ids.reshape(count_blocks, block_boxes, LIST),
             dest_box.reshape(count_blocks, block_boxes, LIST)))
        lifted = lift_each(gathered, two_scale, child_octant)
        parents = jnp.zeros((PARENTS, cube_size), jnp.float32).at[parent_of].add(lifted)
        current = gathered - lift_each(parents[parent_of], flipped, child_octant)
    return current, parents
```

```python
import functools

import jax
import jax.numpy as jnp
from jax import lax
from jax.experimental import pallas as pl
from jax.experimental.pallas import tpu as pltpu
from jax.sharding import PartitionSpec as P

F32, BF16, I32 = jnp.float32, jnp.bfloat16, jnp.int32
K = 16
PLANE = K * K
BOXES = 16
ROWS = BOXES * K
TERMS = 20
SHIFTS = 9
LIST = 16
DEVICES = 128
GROUP = 64
CAP = 2
SLOTS = DEVICES * CAP
WIDE = SHIFTS * PLANE
VMEM_LIMIT = 66_000_000


def mm(a, b):
    return jnp.dot(a, b, preferred_element_type=F32)


def split(a):
    hi = a.astype(BF16)
    return hi, (a - hi.astype(F32)).astype(BF16)


def mm3(a, b):
    a_hi, a_lo = split(a)
    b_hi, b_lo = split(b)
    return mm(a_hi, b_hi) + (mm(a_hi, b_lo) + mm(a_lo, b_hi))


def exact(a, b):
    return jnp.dot(a, b, precision=lax.Precision.HIGHEST, preferred_element_type=F32)


def iotas(shape):
    return lax.broadcasted_iota(I32, shape, 0), lax.broadcasted_iota(I32, shape, 1)


def spreads():
    row, col = iotas((ROWS, K))
    high, low = (row // K == col).astype(F32), (row % K == col).astype(F32)
    row, col = iotas((K, ROWS))
    high_t, low_t = (col // K == row).astype(F32), (col % K == row).astype(F32)
    return high, low, high_t, low_t


def build_source(current, potential, table):
    high, low, high_t, low_t = spreads()
    row, col = iotas((ROWS, ROWS))
    table_t = table.T
    hh = exact(exact(high, table), high_t)
    ll = exact(exact(low, table), low_t)
    hh_t = exact(exact(high, table_t), high_t)
    ll_t = exact(exact(low, table_t), low_t)
    lh_t = exact(exact(low, table_t), high_t)
    left = jnp.where(row % K == col % K, hh, 0.0)
    left_back = jnp.where(row // K == col % K, lh_t, 0.0)
    values = mm3(left, mm3(current, hh_t * ll_t))
    product = values * (potential + 0.25 * values * values)
    return mm3(left_back, mm3(product, hh * ll)).astype(BF16)


def rows_of(ref):
    return jnp.concatenate([ref[:, x * PLANE : (x + 1) * PLANE] for x in range(K)], axis=0)


def start_yz(yz_hbm, yz_buf, sems):
    for m in range(TERMS):
        pltpu.make_async_copy(
            yz_hbm.at[:, m * WIDE : (m + 1) * WIDE], yz_buf.at[m], sems.at[m]
        ).start()


def convolve(source, xk_ref, yz_hbm, yz_buf, partial, conv, sems):
    def first(m, carry):
        pltpu.make_async_copy(yz_hbm.at[:, pl.ds(0, WIDE)], yz_buf.at[m], sems.at[m]).wait()
        at = pl.multiple_of(m * K, K)
        for p in range(SHIFTS):
            part = mm(source, yz_buf[m, :, p * PLANE : (p + 1) * PLANE])
            partial[p * BOXES : (p + 1) * BOXES, pl.ds(at, K), :] = part.astype(BF16).reshape(
                BOXES, K, PLANE
            )
        return carry

    lax.fori_loop(0, TERMS, first, 0)
    xk = xk_ref[...]

    def second(q, carry):
        out = mm(xk, partial[q])
        conv[pl.ds(q * 3, 3)] = out.astype(BF16).reshape(3, K, PLANE)
        return carry

    lax.fori_loop(0, SHIFTS * BOXES, second, 0, unroll=4)


def pick(conv, slot_ref, send_ref):
    def one(j, carry):
        send_ref[j] = conv[slot_ref[j]]
        return carry

    lax.fori_loop(0, SLOTS, one, 0, unroll=8)


def route(dest_ref, disp_ref, parent_ref, group_base, slot_ref, label_ref, up_ref, count):
    def clear(d, carry):
        count[d] = 0
        for c in range(CAP):
            slot_ref[d * CAP + c] = 0
            label_ref[d * CAP + c] = BOXES
        return carry

    lax.fori_loop(0, DEVICES, clear, 0)

    def clear_up(d, carry):
        up_ref[d] = 2 * BOXES
        return carry

    lax.fori_loop(0, GROUP, clear_up, 0)

    def one(j, carry):
        box, slot = j // LIST, j % LIST
        dest = dest_ref[box, slot]

        @pl.when(dest >= 0)
        def _():
            disp = disp_ref[box, slot]
            along_x = (disp * 57) // 512
            owner = dest // BOXES
            rank = count[owner]
            count[owner] = rank + 1
            slot_ref[owner * CAP + rank] = ((disp - SHIFTS * along_x) * BOXES + box) * 3 + along_x
            label_ref[owner * CAP + rank] = dest % BOXES

        return carry

    lax.fori_loop(0, BOXES * LIST, one, 0)

    def climb(box, carry):
        local = parent_ref[box] - group_base
        up_ref[local // 2] = box * 2 + local % 2
        return carry

    lax.fori_loop(0, BOXES, climb, 0)


def first_kernel(
    dest_ref, disp_ref, parent_ref, coef_ref, pot_ref, table_ref, xk_ref, yz_hbm,
    send_ref, slot_ref, label_ref, up_ref, yz_buf, partial, conv, count, sems,
):
    start_yz(yz_hbm, yz_buf, sems)
    route(
        dest_ref, disp_ref, parent_ref, (parent_ref[0] // 128) * 128,
        slot_ref, label_ref, up_ref, count,
    )
    source = build_source(rows_of(coef_ref), rows_of(pot_ref), table_ref[...])
    convolve(source, xk_ref, yz_hbm, yz_buf, partial, conv, sems)
    pick(conv, slot_ref, send_ref)


def octant_rows(octant_ref, order):
    row, col = iotas((ROWS, BOXES))
    hit = (row // K if order == "high" else row % K) == col
    return jnp.sum(jnp.where(hit, octant_ref[...], 0), axis=1, keepdims=True)


def by_octant(blocks, octants, half, high_filters, low_filters):
    out = jnp.zeros((ROWS, PLANE), F32)
    for c in range(4):
        quad = (high_filters[c // 2] * low_filters[c % 2]).astype(BF16)
        out = jnp.where(octants % 4 == c, mm(blocks, quad), out)
    return out


def gather_kernel(label_ref, up_ref, recv_ref, scale_ref, octant_ref, gathered_ref, up_send, acc, lifted):
    acc[...] = jnp.zeros_like(acc)

    def one(j, carry):
        c = label_ref[j]
        acc[c] = acc[c] + recv_ref[j].astype(F32)
        return carry

    lax.fori_loop(0, SLOTS, one, 0, unroll=8)
    gathered = acc[:BOXES].reshape(ROWS, PLANE)
    gathered_ref[...] = gathered
    high, low, high_t, low_t = spreads()
    row, col = iotas((ROWS, ROWS))
    filters_t = [scale_ref[c].T for c in range(2)]
    high_filters = [exact(exact(high, f), high_t) for f in filters_t]
    low_filters = [exact(exact(low, f), low_t) for f in filters_t]
    octants = octant_rows(octant_ref, "high")
    inner = by_octant(gathered.astype(BF16), octants, PLANE, high_filters, low_filters)
    lefts = [exact(exact(low, scale_ref[c]), low_t) for c in range(2)]
    left = jnp.where(octants // 4 == 1, lefts[1], lefts[0])
    left = jnp.where(row // K == col // K, left, 0.0)
    out = mm(left.astype(BF16), inner.astype(BF16))
    lifted[...] = out.astype(BF16).reshape(BOXES, K, PLANE)

    def send(d, carry):
        up_send[d] = lifted[jnp.minimum(up_ref[d] // 2, BOXES - 1)]
        return carry

    lax.fori_loop(0, GROUP, send, 0, unroll=8)


def parent_kernel(up_label_ref, recv_ref, parents_ref, down_ref, acc, rounded):
    acc[...] = jnp.zeros_like(acc)

    def one(d, carry):
        p = up_label_ref[d]
        acc[p] = acc[p] + recv_ref[d].astype(F32)
        return carry

    lax.fori_loop(0, GROUP, one, 0, unroll=8)
    for p in range(2):
        for i in range(K):
            parents_ref[p : p + 1, i * PLANE : (i + 1) * PLANE] = acc[p, i : i + 1, :]
    rounded[...] = acc[:2].astype(BF16)

    def send(d, carry):
        down_ref[d] = rounded[jnp.minimum(up_label_ref[d], 1)]
        return carry

    lax.fori_loop(0, GROUP, send, 0, unroll=8)


def corrected(parent_ref, down_ref, gathered_ref, scale_ref, octant_ref, matched):
    group_base = (parent_ref[0] // 128) * 128

    def one(b, carry):
        matched[b] = down_ref[(parent_ref[b] - group_base) // 2]
        return carry

    lax.fori_loop(0, BOXES, one, 0, unroll=4)
    high, low, high_t, low_t = spreads()
    row, col = iotas((ROWS, ROWS))
    high_filters = [exact(exact(high, scale_ref[c]), high_t) for c in range(2)]
    low_filters = [exact(exact(low, scale_ref[c]), low_t) for c in range(2)]
    octants = octant_rows(octant_ref, "high")
    inner = by_octant(
        matched[...].reshape(ROWS, PLANE), octants, PLANE, high_filters, low_filters
    )
    lefts = [exact(exact(high, scale_ref[c].T), low_t) for c in range(2)]
    left = jnp.where(octant_rows(octant_ref, "low") // 4 == 1, lefts[1], lefts[0])
    same = row % K == col // K
    left = jnp.where(same, left, 0.0)
    swap = jnp.where(same & (row // K == col % K), 1.0, 0.0).astype(BF16)
    g_hi, g_lo = split(gathered_ref[...])
    return mm(swap, g_hi) + mm(swap, g_lo) - mm(left.astype(BF16), inner.astype(BF16))


def again_kernel(
    slot_ref, parent_ref, down_ref, gathered_ref, scale_ref, octant_ref, pot_ref, table_ref, xk_ref, yz_hbm,
    send_ref, yz_buf, partial, conv, matched, sems,
):
    start_yz(yz_hbm, yz_buf, sems)
    current = corrected(parent_ref, down_ref, gathered_ref, scale_ref, octant_ref, matched)
    source = build_source(current, rows_of(pot_ref), table_ref[...])
    convolve(source, xk_ref, yz_hbm, yz_buf, partial, conv, sems)
    pick(conv, slot_ref, send_ref)


def last_kernel(parent_ref, down_ref, gathered_ref, scale_ref, octant_ref, out_ref, matched):
    current = corrected(parent_ref, down_ref, gathered_ref, scale_ref, octant_ref, matched)
    for x in range(K):
        out_ref[:, x * PLANE : (x + 1) * PLANE] = current[x * BOXES : (x + 1) * BOXES, :]


SMEM = pl.BlockSpec(memory_space=pltpu.SMEM)
VMEM = pl.BlockSpec(memory_space=pltpu.VMEM)
ANY = pl.BlockSpec(memory_space=pl.ANY)


def call(kernel, outs, out_specs, in_specs, scratch, *args, limit=None):
    return pl.pallas_call(
        kernel,
        out_shape=outs,
        in_specs=in_specs,
        out_specs=out_specs,
        scratch_shapes=scratch,
        compiler_params=pltpu.CompilerParams(vmem_limit_bytes=limit),
    )(*args)


def tiles(count, kind=BF16):
    return jax.ShapeDtypeStruct((count, K, PLANE), kind)


def ints(count):
    return jax.ShapeDtypeStruct((count,), I32)


def shards(
    coefficients,
    potential,
    to_values,
    x_kernels,
    yz_kernels,
    two_scale,
    disp_ids,
    dest_box,
    parent_of,
    child_octant,
):
    xk = x_kernels.transpose(1, 0, 2).reshape(3 * K, TERMS * K)
    octant = child_octant.reshape(1, BOXES)
    heavy = [
        pltpu.VMEM((TERMS, PLANE, WIDE), BF16),
        pltpu.VMEM((SHIFTS * BOXES, TERMS * K, PLANE), BF16),
        pltpu.VMEM((SHIFTS * BOXES * 3, K, PLANE), BF16),
    ]
    everyone = ("oct", "sub")
    swap = functools.partial(lax.all_to_all, split_axis=0, concat_axis=0, tiled=True)
    send, slots, labels, ups = call(
        first_kernel,
        (tiles(SLOTS), ints(SLOTS), ints(SLOTS), ints(GROUP)),
        (VMEM, SMEM, SMEM, SMEM),
        [SMEM] * 3 + [VMEM] * 4 + [ANY],
        heavy + [pltpu.SMEM((DEVICES,), I32), pltpu.SemaphoreType.DMA((TERMS,))],
        dest_box, disp_ids, parent_of, coefficients, potential, to_values, xk, yz_kernels,
        limit=VMEM_LIMIT,
    )
    up_out = jnp.where(ups >= 2 * BOXES, 2, ups % 2)
    box_labels = swap(labels.astype(BF16).reshape(DEVICES, CAP), everyone).reshape(-1).astype(I32)
    up_labels = swap(up_out.astype(BF16).reshape(GROUP, 1), "sub").reshape(-1).astype(I32)
    for iteration in range(2):
        recv = swap(send, everyone)
        gathered, up_send = call(
            gather_kernel,
            (jax.ShapeDtypeStruct((ROWS, PLANE), F32), tiles(GROUP)),
            (VMEM, VMEM),
            [SMEM, SMEM, VMEM, VMEM, VMEM],
            [pltpu.VMEM((BOXES + 1, K, PLANE), F32), pltpu.VMEM((BOXES, K, PLANE), BF16)],
            box_labels, ups, recv, two_scale, octant,
        )
        up_recv = swap(up_send, "sub")
        parents, down_send = call(
            parent_kernel,
            (jax.ShapeDtypeStruct((2, K * PLANE), F32), tiles(GROUP)),
            (VMEM, VMEM),
            [SMEM, VMEM],
            [pltpu.VMEM((3, K, PLANE), F32), pltpu.VMEM((2, K, PLANE), BF16)],
            up_labels, up_recv,
        )
        down_recv = swap(down_send, "sub")
        matched = pltpu.VMEM((BOXES, K, PLANE), BF16)
        if iteration == 0:
            send = call(
                again_kernel,
                tiles(SLOTS),
                VMEM,
                [SMEM] * 2 + [VMEM] * 7 + [ANY],
                heavy + [matched, pltpu.SemaphoreType.DMA((TERMS,))],
                slots, parent_of, down_recv, gathered, two_scale, octant, potential, to_values, xk, yz_kernels,
                limit=VMEM_LIMIT,
            )
        else:
            field = call(
                last_kernel,
                jax.ShapeDtypeStruct((BOXES, K * PLANE), F32),
                VMEM,
                [SMEM] + [VMEM] * 4,
                [matched],
                parent_of, down_recv, gathered, two_scale, octant,
            )
    return field, parents


def solution(mesh):
    spread = P(("oct", "sub"), None)
    placed = (spread, spread, P(), P(), P(), P(), spread, spread, P(("oct", "sub")), P(("oct", "sub")))
    return jax.shard_map(
        shards, mesh=mesh, in_specs=placed, out_specs=(spread, spread), check_vma=False
    )
```

```python
import functools

import jax
import jax.numpy as jnp
from jax import lax
from jax.experimental import pallas as pl
from jax.experimental.pallas import tpu as pltpu
from jax.sharding import PartitionSpec as P

F32, BF16, I32 = jnp.float32, jnp.bfloat16, jnp.int32
MESH = pl.DeviceIdType.MESH
ITERS = 2
K = 16
PLANE = K * K
BOXES = 16
ROWS = BOXES * K
TERMS = 20
SHIFTS = 9
LIST = 16
DEVICES = 128
GROUP = 64
CAP = 2
SLOTS = DEVICES * CAP
WIDE = SHIFTS * PLANE
SIDE = 4
STRIDE, UNSTRIDE = 37, 45
BURST = 4
BATCH = 8
UP_BATCH = 16
NO_PARENT = 2
VMEM_LIMIT = 67_000_000


def mm(a, b):
    return jnp.dot(a, b, preferred_element_type=F32)


def split(a):
    hi = a.astype(BF16)
    return hi, (a - hi.astype(F32)).astype(BF16)


def mm3(a, b):
    return mm(a[0], b[0]) + (mm(a[0], b[1]) + mm(a[1], b[0]))


def exact(a, b):
    return jnp.dot(a, b, precision=lax.Precision.HIGHEST, preferred_element_type=F32)


def iotas(shape):
    return lax.broadcasted_iota(I32, shape, 0), lax.broadcasted_iota(I32, shape, 1)


def spreads():
    row, col = iotas((ROWS, K))
    high, low = (row // K == col).astype(F32), (row % K == col).astype(F32)
    row, col = iotas((K, ROWS))
    high_t, low_t = (col // K == row).astype(F32), (col % K == row).astype(F32)
    return high, low, high_t, low_t


def fill_values(table, mats):
    high, low, high_t, low_t = spreads()
    row, col = iotas((ROWS, ROWS))
    table_t = table.T
    hh = exact(exact(high, table), high_t)
    ll = exact(exact(low, table), low_t)
    hh_t = exact(exact(high, table_t), high_t)
    ll_t = exact(exact(low, table_t), low_t)
    lh_t = exact(exact(low, table_t), high_t)
    left = jnp.where(row % K == col % K, hh, 0.0)
    left_back = jnp.where(row // K == col % K, lh_t, 0.0)
    for n, mat in enumerate((left, hh_t * ll_t, left_back, hh * ll)):
        hi, lo = split(mat)
        mats[2 * n] = hi
        mats[2 * n + 1] = lo


def octant_rows(octant_ref, digit):
    row, col = iotas((ROWS, BOXES))
    hit = (row // K if digit == "high" else row % K) == col
    return jnp.sum(jnp.where(hit, octant_ref[...], 0), axis=1, keepdims=True)


def fill_tree(scale_ref, octant_ref, up_mats, down_mats, sides):
    high, low, high_t, low_t = spreads()
    row, col = iotas((ROWS, ROWS))
    filters = [scale_ref[c] for c in range(2)]
    turned = [f.T for f in filters]
    for mats, pair in ((up_mats, turned), (down_mats, filters)):
        highs = [exact(exact(high, f), high_t) for f in pair]
        lows = [exact(exact(low, f), low_t) for f in pair]
        for c in range(4):
            mats[c] = (highs[c // 2] * lows[c % 2]).astype(BF16)
    ups = [exact(exact(low, f), low_t) for f in filters]
    up = jnp.where(octant_rows(octant_ref, "high") // 4 == 1, ups[1], ups[0])
    sides[0] = jnp.where(row // K == col // K, up, 0.0).astype(BF16)
    downs = [exact(exact(high, f), low_t) for f in turned]
    down = jnp.where(octant_rows(octant_ref, "low") // 4 == 1, downs[1], downs[0])
    same = row % K == col // K
    sides[1] = jnp.where(same, down, 0.0).astype(BF16)
    sides[2] = jnp.where(same & (row // K == col % K), 1.0, 0.0).astype(BF16)


def by_octant(blocks, octants, mats):
    out = mm(blocks, mats[0])
    for c in range(1, 4):
        out = jnp.where(octants == c, mm(blocks, mats[c]), out)
    return out


def source_of(current, pot_ref, mats):
    pairs = [(mats[2 * n], mats[2 * n + 1]) for n in range(4)]
    values = mm3(pairs[0], split(mm3(split(current), pairs[1])))
    product = values * (rows_of(pot_ref) + 0.25 * values * values)
    return mm3(pairs[2], split(mm3(split(product), pairs[3]))).astype(BF16)


def rows_of(ref):
    return jnp.concatenate([ref[:, x * PLANE : (x + 1) * PLANE] for x in range(K)], axis=0)


def place():
    sub = lax.axis_index("sub")
    return lax.axis_index("oct"), sub // (SIDE * SIDE), (sub // SIDE) % SIDE, sub % SIDE


def partner(order, sign):
    core, x, z, y = place()
    k = lax.rem((order // 2) * STRIDE, GROUP)
    step = GROUP if sign < 0 else 0
    x = lax.rem(x + sign * (k // 16) + step, SIDE)
    z = lax.rem(z + sign * lax.rem(k // SIDE, SIDE) + step, SIDE)
    y = lax.rem(y + sign * lax.rem(k, SIDE) + step, SIDE)
    return (lax.rem(core + lax.rem(order, 2), 2), (x * SIDE + z) * SIDE + y)


def route_kernel(
    me_ref, dest_ref, disp_ref, parent_ref, plane_ref, shift_ref, child_ref, home_ref, labels_ref, count, label, up,
):
    core, sub = me_ref[0], me_ref[1]
    x, z, y = sub // 16, (sub // SIDE) % SIDE, sub % SIDE

    def order_of(other_core, other):
        kx = lax.rem(other // 16 - x + SIDE, SIDE)
        kz = lax.rem(lax.rem(other // SIDE, SIDE) - z + SIDE, SIDE)
        ky = lax.rem(lax.rem(other, SIDE) - y + SIDE, SIDE)
        u = lax.rem(((kx * SIDE + kz) * SIDE + ky) * UNSTRIDE, GROUP)
        return 2 * u + lax.rem(other_core - core + 2, 2)

    def clear(d, carry):
        count[d] = 0
        up[d] = NO_PARENT
        for c in range(CAP):
            plane_ref[d * CAP + c] = 0
            shift_ref[d * CAP + c] = 0
            label[d * CAP + c] = BOXES
        return carry

    lax.fori_loop(0, DEVICES, clear, 0)

    def clear_child(d, carry):
        child_ref[d] = 0
        return carry

    lax.fori_loop(0, GROUP, clear_child, 0)

    def one(j, carry):
        box, slot = j // LIST, lax.rem(j, LIST)
        dest = dest_ref[box, slot]

        @pl.when(dest >= 0)
        def _():
            disp = disp_ref[box, slot]
            along_x = (disp * 57) // 512
            order = order_of(dest // (BOXES * GROUP), lax.rem(dest // BOXES, GROUP))
            rank = count[order]
            count[order] = rank + 1
            at = order * CAP + rank
            plane_ref[at] = (disp - SHIFTS * along_x) * BOXES + box
            shift_ref[at] = along_x
            label[at] = lax.rem(dest, BOXES)

        return carry

    lax.fori_loop(0, BOXES * LIST, one, 0)

    def climb(box, carry):
        parent = lax.rem(parent_ref[box], 2 * GROUP)
        order = order_of(core, parent // 2)
        up[order] = lax.rem(parent, 2)
        child_ref[order // 2] = box
        home_ref[box] = order // 2
        return carry

    lax.fori_loop(0, BOXES, climb, 0)
    first = (lax.broadcasted_iota(I32, (1, PLANE), 1) // K) % 2 == 0

    def row(d, carry):
        both = jnp.where(first, label[d * CAP], label[d * CAP + 1])
        labels_ref[d] = both + 32 * up[d]
        return carry

    lax.fori_loop(0, DEVICES, row, 0, unroll=8)


def main_kernel(
    plane_ref, shift_ref, child_ref, home_ref,
    labels_ref, coef_ref, pot_ref, table_ref, scale_ref, octant_ref, xk_ref, yz_hbm,
    field_ref, parents_ref,
    yz_buf, partial, send, recv, up_send, up_recv, down_send, down_recv, tags,
    mats, up_mats, down_mats, sides, lifted, matched,
    yz_sem, tag_sem, send_sem, recv_sem, tree_sem,
):
    for m in range(TERMS):
        pltpu.make_async_copy(
            yz_hbm.at[:, m * WIDE : (m + 1) * WIDE], yz_buf.at[m], yz_sem.at[m]
        ).start()
    barrier = pltpu.get_barrier_semaphore()

    def greet(j, carry):
        pl.semaphore_signal(barrier, inc=1, device_id=partner(j, 1), device_id_type=MESH)
        return carry

    lax.fori_loop(1, DEVICES, greet, 0)

    def remote(source, target, out_sem, in_sem, device):
        return pltpu.make_async_remote_copy(
            src_ref=source, dst_ref=target, send_sem=out_sem, recv_sem=in_sem,
            device_id=device, device_id_type=MESH,
        )

    def arrived(region, out_sem, in_sem):
        remote(region, region, out_sem, in_sem, partner(1, 1)).wait_recv()

    def left(region, out_sem, in_sem):
        remote(region, region, out_sem, in_sem, partner(1, 1)).wait_send()

    fill_values(table_ref[...], mats)
    source = source_of(rows_of(coef_ref), pot_ref, mats)
    fill_tree(scale_ref, octant_ref, up_mats, down_mats, sides)
    octants = octant_rows(octant_ref, "high") % 4
    row, col = iotas((ROWS, ROWS))
    same_plane = row % K == col % K
    row_box = row // K

    for it in range(ITERS):

        def first(m, carry, it=it, source=source):
            if it == 0:
                pltpu.make_async_copy(
                    yz_hbm.at[:, pl.ds(0, WIDE)], yz_buf.at[m], yz_sem.at[m]
                ).wait()
            at = pl.multiple_of(m * K, K)
            for p in range(SHIFTS):
                part = mm(source, yz_buf[m, :, p * PLANE : (p + 1) * PLANE])
                partial[p * BOXES : (p + 1) * BOXES, pl.ds(at, K), :] = part.astype(BF16).reshape(
                    BOXES, K, PLANE
                )
            return carry

        lax.fori_loop(0, TERMS, first, 0)

        if it == 0:
            pl.semaphore_wait(barrier, DEVICES - 1)

            def tell(j, carry):
                remote(labels_ref.at[j], tags.at[j], tag_sem.at[0], tag_sem.at[1], partner(j, 1)).start()
                return carry

            lax.fori_loop(1, DEVICES, tell, 0)
            tags[0] = labels_ref[0]
        else:
            left(send.at[pl.ds(1, DEVICES - 1)], send_sem.at[it - 1], recv_sem.at[0, 0])

        def ship(j, it=it):
            batch = j // BATCH
            return remote(
                send.at[j], recv.at[it, j], send_sem.at[it], recv_sem.at[it, batch], partner(j, 1)
            )

        def burst(n, carry, it=it, ship=ship):
            for e in range(BURST):
                before = (n - 1) * BURST + e

                @pl.when(before >= 1)
                def _():
                    ship(before).start()

            for e in range(BURST):
                for c in range(CAP):
                    at = (n * BURST + e) * CAP + c
                    tile = mm(xk_ref[shift_ref[at]], partial[plane_ref[at]])
                    send[n * BURST + e, c] = tile.astype(BF16)
            return carry

        bursts = DEVICES // BURST
        lax.fori_loop(0, bursts, burst, 0)
        for e in range(BURST):
            ship((bursts - 1) * BURST + e).start()
        recv[it, 0] = send[0]

        if it == 0:
            arrived(tags.at[pl.ds(1, DEVICES - 1)], tag_sem.at[0], tag_sem.at[1])

        gathered = jnp.zeros((ROWS, PLANE), F32)
        for g in range(DEVICES // BATCH):
            lo = max(1, g * BATCH)
            arrived(
                recv.at[it, pl.ds(lo, (g + 1) * BATCH - lo)], send_sem.at[it], recv_sem.at[it, g]
            )
            marks = tags[g * BATCH : (g + 1) * BATCH].reshape(BATCH, PLANE) % 32
            row8, col8 = iotas((BATCH, PLANE))
            marks = jnp.sum(
                jnp.where(row8 == col8 // (CAP * K), marks, 0), axis=0, keepdims=True
            )
            member = jnp.where(same_plane & (marks == row_box), 1.0, 0.0).astype(BF16)
            block = recv[it, g * BATCH : (g + 1) * BATCH].reshape(ROWS, PLANE)
            gathered = gathered + mm(member, block)

        inner = by_octant(gathered.astype(BF16), octants, up_mats)
        up = mm(sides[0], inner.astype(BF16))
        lifted[...] = up.astype(BF16).reshape(BOXES, K, PLANE)

        def fill_up(u, carry):
            up_send[u] = lifted[child_ref[u]]
            return carry

        if it > 0:
            left(up_send.at[pl.ds(1, GROUP - 1)], tree_sem.at[it - 1, 0], tree_sem.at[0, 1])
        lax.fori_loop(0, GROUP, fill_up, 0, unroll=8)

        def ship_up(u, carry, it=it):
            remote(
                up_send.at[u], up_recv.at[it, u], tree_sem.at[it, 0], tree_sem.at[it, 1],
                partner(2 * u, 1),
            ).start()
            return carry

        lax.fori_loop(1, GROUP, ship_up, 0)
        up_recv[it, 0] = up_send[0]
        arrived(up_recv.at[it, pl.ds(1, GROUP - 1)], tree_sem.at[it, 0], tree_sem.at[it, 1])

        sums = jnp.zeros((2 * K, PLANE), F32)
        row_p, col_p = iotas((2 * K, PLANE))
        for h in range(GROUP // UP_BATCH):
            span = 2 * UP_BATCH
            marks = tags[h * span : (h + 1) * span].reshape(span, PLANE) // 32
            row_s, col_s = iotas((span, PLANE))
            marks = jnp.sum(jnp.where(row_s == 2 * (col_s // K), marks, 0), axis=0, keepdims=True)
            member = jnp.where((row_p % K == col_p % K) & (marks == row_p // K), 1.0, 0.0)
            block = up_recv[it, h * UP_BATCH : (h + 1) * UP_BATCH].reshape(ROWS, PLANE)
            sums = sums + mm(member.astype(BF16), block)
        if it == ITERS - 1:
            for p in range(2):
                for i in range(K):
                    at = p * K + i
                    parents_ref[p : p + 1, i * PLANE : (i + 1) * PLANE] = sums[at : at + 1, :]

        if it > 0:
            left(down_send.at[pl.ds(1, GROUP - 1)], tree_sem.at[it - 1, 2], tree_sem.at[0, 3])

        def fill_down(u, carry, sums=sums):
            second = tags[2 * u] // 32 == 1
            down_send[u] = jnp.where(second, sums[K:], sums[:K]).astype(BF16)
            return carry

        lax.fori_loop(0, GROUP, fill_down, 0, unroll=8)

        def ship_down(u, carry, it=it):
            remote(
                down_send.at[u], down_recv.at[it, u], tree_sem.at[it, 2], tree_sem.at[it, 3],
                partner(2 * u, -1),
            ).start()
            return carry

        lax.fori_loop(1, GROUP, ship_down, 0)
        down_recv[it, 0] = down_send[0]
        arrived(down_recv.at[it, pl.ds(1, GROUP - 1)], tree_sem.at[it, 2], tree_sem.at[it, 3])

        for b in range(BOXES):
            matched[b] = down_recv[it, home_ref[b]]
        inner = by_octant(matched[...].reshape(ROWS, PLANE), octants, down_mats)
        g_hi, g_lo = split(gathered)
        current = mm(sides[2], g_hi) + mm(sides[2], g_lo) - mm(sides[1], inner.astype(BF16))
        if it < ITERS - 1:
            source = source_of(current, pot_ref, mats)
        else:
            for x in range(K):
                field_ref[:, x * PLANE : (x + 1) * PLANE] = current[x * BOXES : (x + 1) * BOXES, :]

    last = ITERS - 1
    left(tags.at[pl.ds(1, DEVICES - 1)], tag_sem.at[0], tag_sem.at[1])
    left(send.at[pl.ds(1, DEVICES - 1)], send_sem.at[last], recv_sem.at[0, 0])
    left(up_send.at[pl.ds(1, GROUP - 1)], tree_sem.at[last, 0], tree_sem.at[0, 1])
    left(down_send.at[pl.ds(1, GROUP - 1)], tree_sem.at[last, 2], tree_sem.at[0, 3])


SMEM = pl.BlockSpec(memory_space=pltpu.SMEM)
VMEM = pl.BlockSpec(memory_space=pltpu.VMEM)
ANY = pl.BlockSpec(memory_space=pl.ANY)


def shards(
    coefficients,
    potential,
    to_values,
    x_kernels,
    yz_kernels,
    two_scale,
    disp_ids,
    dest_box,
    parent_of,
    child_octant,
):
    xk = x_kernels.transpose(1, 0, 2).reshape(3, K, TERMS * K)
    octant = child_octant.reshape(1, BOXES)
    me = jnp.stack([lax.axis_index("oct"), lax.axis_index("sub")]).astype(I32)
    ints = functools.partial(jax.ShapeDtypeStruct, dtype=I32)
    planes, shifts, children, homes, labels = pl.pallas_call(
        route_kernel,
        out_shape=(ints((SLOTS,)), ints((SLOTS,)), ints((GROUP,)), ints((BOXES,)), ints((DEVICES, 1, PLANE))),
        in_specs=[SMEM] * 4,
        out_specs=(SMEM, SMEM, SMEM, SMEM, VMEM),
        scratch_shapes=[
            pltpu.SMEM((DEVICES,), I32),
            pltpu.SMEM((SLOTS,), I32),
            pltpu.SMEM((DEVICES,), I32),
        ],
    )(me, dest_box, disp_ids, parent_of)
    mat = (ROWS, ROWS)
    dma = pltpu.SemaphoreType.DMA
    return pl.pallas_call(
        main_kernel,
        out_shape=(
            jax.ShapeDtypeStruct((BOXES, K * PLANE), F32),
            jax.ShapeDtypeStruct((2, K * PLANE), F32),
        ),
        in_specs=[SMEM] * 4 + [VMEM] * 7 + [ANY],
        out_specs=(VMEM, VMEM),
        scratch_shapes=[
            pltpu.VMEM((TERMS, PLANE, WIDE), BF16),
            pltpu.VMEM((SHIFTS * BOXES, TERMS * K, PLANE), BF16),
            pltpu.VMEM((DEVICES, CAP, K, PLANE), BF16),
            pltpu.VMEM((ITERS, DEVICES, CAP, K, PLANE), BF16),
            pltpu.VMEM((GROUP, K, PLANE), BF16),
            pltpu.VMEM((ITERS, GROUP, K, PLANE), BF16),
            pltpu.VMEM((GROUP, K, PLANE), BF16),
            pltpu.VMEM((ITERS, GROUP, K, PLANE), BF16),
            pltpu.VMEM((DEVICES, 1, PLANE), I32),
            pltpu.VMEM((8, *mat), BF16),
            pltpu.VMEM((4, *mat), BF16),
            pltpu.VMEM((4, *mat), BF16),
            pltpu.VMEM((3, *mat), BF16),
            pltpu.VMEM((BOXES, K, PLANE), BF16),
            pltpu.VMEM((BOXES, K, PLANE), BF16),
            dma((TERMS,)),
            dma((2,)),
            dma((ITERS,)),
            dma((ITERS, DEVICES // BATCH)),
            dma((ITERS, 4)),
        ],
        compiler_params=pltpu.CompilerParams(
            vmem_limit_bytes=VMEM_LIMIT, collective_id=0, has_side_effects=True
        ),
    )(
        planes, shifts, children, homes,
        labels, coefficients, potential, to_values, two_scale, octant, xk, yz_kernels,
    )


def solution(mesh):
    spread = P(("oct", "sub"), None)
    placed = (spread, spread, P(), P(), P(), P(), spread, spread, P(("oct", "sub")), P(("oct", "sub")))
    return jax.shard_map(
        shards, mesh=mesh, in_specs=placed, out_specs=(spread, spread), check_vma=False
    )
```

```python
import functools

import jax
import jax.numpy as jnp
from jax import lax
from jax.experimental import pallas as pl
from jax.experimental.pallas import tpu as pltpu
from jax.sharding import PartitionSpec as P

F32, BF16, I32 = jnp.float32, jnp.bfloat16, jnp.int32
MESH = pl.DeviceIdType.MESH
ITERS = 2
K = 16
PLANE = K * K
BOXES = 16
ROWS = BOXES * K
TERMS = 20
SHIFTS = 9
LIST = 16
DEVICES = 128
GROUP = 64
CAP = 2
HALVES, HALF = 2, PLANE // 2
SLOTS = DEVICES * CAP
WIDE = SHIFTS * PLANE
SIDE = 4
BURSTS = GROUP // SIDE
BATCH = DEVICES // BURSTS
UP_BATCH = 16
NO_PARENT = 2
CHILD, HOME, TABLE = 2 * SLOTS, 2 * SLOTS + DEVICES, 2 * SLOTS + 2 * DEVICES
VMEM_LIMIT = 67_000_000


def mm(a, b):
    return jnp.dot(a, b, preferred_element_type=F32)


def split(a):
    hi = a.astype(BF16)
    return hi, (a - hi.astype(F32)).astype(BF16)


def mm3(a, b):
    return mm(a[0], b[0]) + (mm(a[0], b[1]) + mm(a[1], b[0]))


def exact(a, b):
    return jnp.dot(a, b, precision=lax.Precision.HIGHEST, preferred_element_type=F32)


def iotas(shape):
    return lax.broadcasted_iota(I32, shape, 0), lax.broadcasted_iota(I32, shape, 1)


def spreads():
    row, col = iotas((ROWS, K))
    high, low = (row // K == col).astype(F32), (row % K == col).astype(F32)
    row, col = iotas((K, ROWS))
    high_t, low_t = (col // K == row).astype(F32), (col % K == row).astype(F32)
    return high, low, high_t, low_t


def fill_values(table, mats):
    high, low, high_t, low_t = spreads()
    row, col = iotas((ROWS, ROWS))
    table_t = table.T
    hh = exact(exact(high, table), high_t)
    ll = exact(exact(low, table), low_t)
    hh_t = exact(exact(high, table_t), high_t)
    ll_t = exact(exact(low, table_t), low_t)
    lh_t = exact(exact(low, table_t), high_t)
    left = jnp.where(row % K == col % K, hh, 0.0)
    left_back = jnp.where(row // K == col % K, lh_t, 0.0)
    for n, mat in enumerate((left, hh_t * ll_t, left_back, hh * ll)):
        hi, lo = split(mat)
        mats[2 * n] = hi
        mats[2 * n + 1] = lo


def octant_rows(octant_ref, digit):
    row, col = iotas((ROWS, BOXES))
    hit = (row // K if digit == "high" else row % K) == col
    return jnp.sum(jnp.where(hit, octant_ref[...], 0), axis=1, keepdims=True)


def fill_tree(scale_ref, octant_ref, up_mats, down_mats, sides):
    high, low, high_t, low_t = spreads()
    row, col = iotas((ROWS, ROWS))
    filters = [scale_ref[c] for c in range(2)]
    turned = [f.T for f in filters]
    for mats, pair in ((up_mats, turned), (down_mats, filters)):
        highs = [exact(exact(high, f), high_t) for f in pair]
        lows = [exact(exact(low, f), low_t) for f in pair]
        for c in range(4):
            mats[c] = (highs[c // 2] * lows[c % 2]).astype(BF16)
    ups = [exact(exact(low, f), low_t) for f in filters]
    up = jnp.where(octant_rows(octant_ref, "high") // 4 == 1, ups[1], ups[0])
    sides[0] = jnp.where(row // K == col // K, up, 0.0).astype(BF16)
    downs = [exact(exact(high, f), low_t) for f in turned]
    down = jnp.where(octant_rows(octant_ref, "low") // 4 == 1, downs[1], downs[0])
    same = row % K == col // K
    sides[1] = jnp.where(same, down, 0.0).astype(BF16)
    sides[2] = jnp.where(same & (row // K == col % K), 1.0, 0.0).astype(BF16)


def by_octant(blocks, octants, mats):
    out = mm(blocks, mats[0])
    for c in range(1, 4):
        out = jnp.where(octants == c, mm(blocks, mats[c]), out)
    return out


def source_of(current, pot_ref, mats):
    pairs = [(mats[2 * n], mats[2 * n + 1]) for n in range(4)]
    values = mm3(pairs[0], split(mm3(split(current), pairs[1])))
    product = values * (rows_of(pot_ref) + 0.25 * values * values)
    return mm3(pairs[2], split(mm3(split(product), pairs[3]))).astype(BF16)


def rows_of(ref):
    return jnp.concatenate([ref[:, x * PLANE : (x + 1) * PLANE] for x in range(K)], axis=0)


def place():
    sub = lax.axis_index("sub")
    return lax.axis_index("oct"), sub // (SIDE * SIDE), (sub // SIDE) % SIDE, sub % SIDE


def burst_of(n, sign):
    core, x, z, y = place()
    a, kz = n // SIDE, lax.rem(n, SIDE)
    z_part = lax.rem(z + sign * kz + SIDE, SIDE) * SIDE
    chips = []
    for ky in range(SIDE):
        x_part = lax.rem(x + sign * (a + kz + ky) + 3 * SIDE, SIDE) * (SIDE * SIDE)
        chips.append(x_part + z_part + lax.rem(y + sign * ky + SIDE, SIDE))
    cores = (core, 1 - core)
    return [[(cores[c], chips[t]) for c in range(2)] for t in range(SIDE)]


def in_bursts(ship, fill=None):
    if fill is None:
        ship(0, 1)

        def step(n, carry):
            ship(n, 0)
            return carry

        lax.fori_loop(1, BURSTS, step, 0)
        return
    fill(0)
    ship(0, 1)
    fill(1)

    def step(n, carry):
        ship(n - 1, 0)
        fill(n)
        return carry

    lax.fori_loop(2, BURSTS, step, 0)
    ship(BURSTS - 1, 0)


def displacement_order(own, core, sub):
    core_0, x, z, y = own
    kx, kz, ky = (sub // 16 - x) & 3, (sub // SIDE - z) & 3, (sub - y) & 3
    u = (((kx - kz - ky) & 3) * SIDE + kz) * SIDE + ky
    return 2 * u + ((core - core_0) & 1)


def whole(a):
    return (a + 1.5).astype(I32) - 1


def route_kernel(dest_ref, disp_ref, parent_ref, table_ref, labels_ref):
    own = place()
    high, low, high_t, low_t = spreads()
    count = BOXES * LIST

    def as_row(v):
        spread = exact(v.astype(F32), low_t)
        return whole(jnp.sum(jnp.where(high_t > 0.5, spread, 0.0), axis=0, keepdims=True))

    def as_col(v):
        spread = exact(high, v.astype(F32))
        return whole(jnp.sum(jnp.where(low > 0.5, spread, 0.0), axis=1, keepdims=True))

    row, col = iotas((count, count))

    def order_of(dest):
        block = dest >> 4
        order = displacement_order(own, block >> 6, block & (GROUP - 1))
        return jnp.where(dest >= 0, order, -1)

    dest_row, dest_col, disp_col = as_row(dest_ref[...]), as_col(dest_ref[...]), as_col(disp_ref[...])
    order_row, order_col = order_of(dest_row), order_of(dest_col)
    same = order_row == order_col
    rank_row = jnp.sum(jnp.where(same & (row < col), 1, 0), axis=0, keepdims=True)
    rank_col = jnp.sum(jnp.where(same & (col < row), 1, 0), axis=1, keepdims=True)
    at_row = jnp.where(order_row >= 0, order_row * CAP + rank_row, -1)
    at_col = jnp.where(order_col >= 0, order_col * CAP + rank_col, -1)
    along_x = (disp_col * 57) >> 9
    box_col = lax.broadcasted_iota(I32, (count, 1), 0) // LIST
    plane_col = (disp_col - SHIFTS * along_x) * BOXES + box_col
    hit = at_col == col
    table_ref[:, :SLOTS] = jnp.sum(jnp.where(hit, plane_col, 0), axis=0, keepdims=True)
    table_ref[:, SLOTS : 2 * SLOTS] = jnp.sum(jnp.where(hit, along_x, 0), axis=0, keepdims=True)

    parent_row = parent_ref[...] & (2 * GROUP - 1)
    up_row = displacement_order(own, own[0], parent_row >> 1)
    row_b, col_b = iotas((BOXES, BOXES))
    up_col = jnp.sum(jnp.where(row_b == col_b, up_row, 0), axis=1, keepdims=True)
    row_u, col_u = iotas((BOXES, DEVICES))
    children = jnp.sum(jnp.where(up_col == 2 * col_u, row_u, 0), axis=0, keepdims=True)
    table_ref[:, CHILD:HOME] = children
    table_ref[:, HOME : HOME + BOXES] = up_row >> 1

    order, lane = iotas((DEVICES, count))
    which = (dest_row & (BOXES - 1)) - BOXES
    labels = [
        jnp.sum(jnp.where(at_row == order * CAP + c, which, 0), axis=1, keepdims=True) + BOXES
        for c in range(CAP)
    ]
    order_b, lane_b = iotas((DEVICES, BOXES))
    ups = jnp.sum(
        jnp.where(up_row == order_b, (parent_row & 1) - NO_PARENT, 0), axis=1, keepdims=True
    )
    marks = jnp.where((lane // K) % CAP == 0, labels[0], labels[1]) + 32 * (ups + NO_PARENT)
    labels_ref[...] = marks.reshape(DEVICES, 1, PLANE)


def main_kernel(
    slots_ref, labels_ref, coef_ref, pot_ref, table_ref, scale_ref, octant_ref, xk_ref, yz_hbm,
    field_ref, parents_ref,
    yz_buf, partial, send, recv, up_send, up_recv, down_send, down_recv, tags,
    mats, up_mats, down_mats, sides, lifted, matched, xk,
    yz_sem, tag_sem, send_sem, recv_sem, tree_sem,
):
    for m in range(TERMS):
        pltpu.make_async_copy(
            yz_hbm.at[:, m * WIDE : (m + 1) * WIDE], yz_buf.at[m], yz_sem.at[m]
        ).start()
    barrier = pltpu.get_barrier_semaphore()
    someone = burst_of(jnp.int32(0), 1)[1][0]

    def greet(n, skip):
        devices = burst_of(jnp.int32(n), 1)
        for e in range(skip, BATCH):
            pl.semaphore_signal(
                barrier, inc=1, device_id=devices[e // 2][e % 2], device_id_type=MESH
            )

    in_bursts(greet)

    def remote(source, target, out_sem, in_sem, device):
        return pltpu.make_async_remote_copy(
            src_ref=source, dst_ref=target, send_sem=out_sem, recv_sem=in_sem,
            device_id=device, device_id_type=MESH,
        )

    def arrived(region, out_sem, in_sem):
        remote(region, region, out_sem, in_sem, someone).wait_recv()

    def left(region, out_sem, in_sem):
        remote(region, region, out_sem, in_sem, someone).wait_send()

    xk[...] = xk_ref[...].astype(F32).T.astype(BF16).reshape(3, K, TERMS * K)
    fill_values(table_ref[...], mats)
    source = source_of(rows_of(coef_ref), pot_ref, mats)
    octants = octant_rows(octant_ref, "high") % 4
    row, col = iotas((ROWS, ROWS))
    same_plane = row % K == col % K
    row_box = row // K

    pl.semaphore_wait(barrier, DEVICES - 1)

    def tell(n, skip):
        devices = burst_of(jnp.int32(n), 1)
        for e in range(skip, BATCH):
            j = n * BATCH + e
            remote(
                labels_ref.at[j], tags.at[j], tag_sem.at[0], tag_sem.at[1], devices[e // 2][e % 2]
            ).start()

    tell(0, 1)
    tags[0] = labels_ref[0]

    for it in range(ITERS):

        if it > 0:
            left(send.at[:, pl.ds(1, DEVICES - 1)], send_sem.at[it - 1], recv_sem.at[0, 0, 0])
        for h in range(HALVES):
            lanes = slice(h * HALF, (h + 1) * HALF)

            def product(pair, it=it, source=source, h=h, lanes=lanes):
                if it == 0 and h == 0:
                    for e in range(2):
                        m = 2 * pair + e
                        pltpu.make_async_copy(
                            yz_hbm.at[:, pl.ds(0, WIDE)], yz_buf.at[m], yz_sem.at[m]
                        ).wait()
                at = pl.multiple_of(pair * 2 * K, 2 * K)
                for p in range(SHIFTS):
                    lo = p * PLANE + h * HALF
                    both = jnp.concatenate(
                        [yz_buf[2 * pair + e, :, lo : lo + HALF] for e in range(2)], axis=1
                    )
                    part = mm(source, both).astype(BF16)
                    for e in range(2):
                        partial[p * BOXES : (p + 1) * BOXES, pl.ds(at + e * K, K), lanes] = part[
                            :, e * HALF : (e + 1) * HALF
                        ].reshape(BOXES, K, HALF)

            def step(pair, carry, product=product):
                product(pair)
                return carry

            def telling(pair, carry, product=product):
                for e in range(3):
                    tell(1 + 3 * pair + e, 0)
                product(pair)
                return carry

            if it == 0 and h == 0:
                lax.fori_loop(0, BURSTS // 3, telling, 0)
                lax.fori_loop(BURSTS // 3, TERMS // 2, step, 0)
            else:
                lax.fori_loop(0, TERMS // 2, step, 0)

            def ship(n, skip, it=it, h=h):
                devices = burst_of(jnp.int32(n), 1)
                for e in range(skip, BATCH):
                    j = n * BATCH + e
                    remote(
                        send.at[h, j], recv.at[it, h, j], send_sem.at[it], recv_sem.at[it, h, n],
                        devices[e // 2][e % 2],
                    ).start()

            def fill(n, h=h, lanes=lanes):
                for e in range(BATCH):
                    j = n * BATCH + e
                    at = [j * CAP + c for c in range(CAP)]
                    factors = jnp.concatenate([xk[slots_ref[0, SLOTS + i]] for i in at], axis=0)
                    parts = jnp.concatenate([partial[slots_ref[0, i], :, lanes] for i in at], axis=1)
                    both = mm(factors, parts).astype(BF16)
                    for c in range(CAP):
                        send[h, j, c] = both[c * K : (c + 1) * K, c * HALF : (c + 1) * HALF]

            in_bursts(ship, fill)
            recv[it, h, 0] = send[h, 0]

        if it == 0:
            fill_tree(scale_ref, octant_ref, up_mats, down_mats, sides)
        if it == 0:
            arrived(tags.at[pl.ds(1, DEVICES - 1)], tag_sem.at[0], tag_sem.at[1])

        halves = []
        for h in range(HALVES):
            total = jnp.zeros((ROWS, HALF), F32)
            for g in range(BURSTS):
                lo = max(1, g * BATCH)
                arrived(
                    recv.at[it, h, pl.ds(lo, (g + 1) * BATCH - lo)],
                    send_sem.at[it], recv_sem.at[it, h, g],
                )
                marks = tags[g * BATCH : (g + 1) * BATCH].reshape(BATCH, PLANE) % 32
                row8, col8 = iotas((BATCH, PLANE))
                marks = jnp.sum(
                    jnp.where(row8 == col8 // (CAP * K), marks, 0), axis=0, keepdims=True
                )
                member = jnp.where(same_plane & (marks == row_box), 1.0, 0.0).astype(BF16)
                block = recv[it, h, g * BATCH : (g + 1) * BATCH].reshape(ROWS, HALF)
                total = total + mm(member, block)
            halves.append(total)
        gathered = jnp.concatenate(halves, axis=1)

        inner = by_octant(gathered.astype(BF16), octants, up_mats)
        up = mm(sides[0], inner.astype(BF16))
        lifted[...] = up.astype(BF16).reshape(BOXES, K, PLANE)

        if it > 0:
            left(up_send.at[pl.ds(1, GROUP - 1)], tree_sem.at[it - 1, 0], tree_sem.at[0, 1])

        def ship_up(n, skip, it=it):
            devices = burst_of(jnp.int32(n), 1)
            for t in range(skip, SIDE):
                u = n * SIDE + t
                remote(
                    up_send.at[u], up_recv.at[it, u], tree_sem.at[it, 0], tree_sem.at[it, 1],
                    devices[t][0],
                ).start()

        def fill_up(n):
            for t in range(SIDE):
                up_send[n * SIDE + t] = lifted[slots_ref[0, CHILD + n * SIDE + t]]

        in_bursts(ship_up, fill_up)
        up_recv[it, 0] = up_send[0]
        arrived(up_recv.at[it, pl.ds(1, GROUP - 1)], tree_sem.at[it, 0], tree_sem.at[it, 1])

        sums = jnp.zeros((2 * K, PLANE), F32)
        row_p, col_p = iotas((2 * K, PLANE))
        for h in range(GROUP // UP_BATCH):
            span = 2 * UP_BATCH
            marks = tags[h * span : (h + 1) * span].reshape(span, PLANE) // 32
            row_s, col_s = iotas((span, PLANE))
            marks = jnp.sum(jnp.where(row_s == 2 * (col_s // K), marks, 0), axis=0, keepdims=True)
            member = jnp.where((row_p % K == col_p % K) & (marks == row_p // K), 1.0, 0.0)
            block = up_recv[it, h * UP_BATCH : (h + 1) * UP_BATCH].reshape(ROWS, PLANE)
            sums = sums + mm(member.astype(BF16), block)
        if it == ITERS - 1:
            for p in range(2):
                for i in range(K):
                    at = p * K + i
                    parents_ref[p : p + 1, i * PLANE : (i + 1) * PLANE] = sums[at : at + 1, :]

        if it > 0:
            left(down_send.at[pl.ds(1, GROUP - 1)], tree_sem.at[it - 1, 2], tree_sem.at[0, 3])

        def ship_down(n, skip, it=it):
            devices = burst_of(jnp.int32(n), -1)
            for t in range(skip, SIDE):
                u = n * SIDE + t
                remote(
                    down_send.at[u], down_recv.at[it, u], tree_sem.at[it, 2], tree_sem.at[it, 3],
                    devices[t][0],
                ).start()

        def fill_down(n, sums=sums):
            for t in range(SIDE):
                second = tags[2 * (n * SIDE + t)] // 32 == 1
                down_send[n * SIDE + t] = jnp.where(second, sums[K:], sums[:K]).astype(BF16)

        in_bursts(ship_down, fill_down)
        down_recv[it, 0] = down_send[0]
        arrived(down_recv.at[it, pl.ds(1, GROUP - 1)], tree_sem.at[it, 2], tree_sem.at[it, 3])

        for b in range(BOXES):
            matched[b] = down_recv[it, slots_ref[0, HOME + b]]
        inner = by_octant(matched[...].reshape(ROWS, PLANE), octants, down_mats)
        g_hi, g_lo = split(gathered)
        current = mm(sides[2], g_hi) + mm(sides[2], g_lo) - mm(sides[1], inner.astype(BF16))
        if it < ITERS - 1:
            source = source_of(current, pot_ref, mats)
        else:
            for x in range(K):
                field_ref[:, x * PLANE : (x + 1) * PLANE] = current[x * BOXES : (x + 1) * BOXES, :]

    last = ITERS - 1
    left(tags.at[pl.ds(1, DEVICES - 1)], tag_sem.at[0], tag_sem.at[1])
    left(send.at[:, pl.ds(1, DEVICES - 1)], send_sem.at[last], recv_sem.at[0, 0, 0])
    left(up_send.at[pl.ds(1, GROUP - 1)], tree_sem.at[last, 0], tree_sem.at[0, 1])
    left(down_send.at[pl.ds(1, GROUP - 1)], tree_sem.at[last, 2], tree_sem.at[0, 3])


SMEM = pl.BlockSpec(memory_space=pltpu.SMEM)
VMEM = pl.BlockSpec(memory_space=pltpu.VMEM)
ANY = pl.BlockSpec(memory_space=pl.ANY)


def shards(
    coefficients,
    potential,
    to_values,
    x_kernels,
    yz_kernels,
    two_scale,
    disp_ids,
    dest_box,
    parent_of,
    child_octant,
):
    xk = x_kernels.transpose(0, 2, 1).reshape(TERMS * K, 3 * K)
    octant = child_octant.reshape(1, BOXES)
    ints = functools.partial(jax.ShapeDtypeStruct, dtype=I32)
    slots, labels = pl.pallas_call(
        route_kernel,
        out_shape=(ints((1, TABLE)), ints((DEVICES, 1, PLANE))),
        in_specs=[VMEM] * 3,
        out_specs=(VMEM, VMEM),
    )(dest_box, disp_ids, parent_of.reshape(1, BOXES))
    mat = (ROWS, ROWS)
    dma = pltpu.SemaphoreType.DMA
    return pl.pallas_call(
        main_kernel,
        out_shape=(
            jax.ShapeDtypeStruct((BOXES, K * PLANE), F32),
            jax.ShapeDtypeStruct((2, K * PLANE), F32),
        ),
        in_specs=[SMEM] + [VMEM] * 7 + [ANY],
        out_specs=(VMEM, VMEM),
        scratch_shapes=[
            pltpu.VMEM((TERMS, PLANE, WIDE), BF16),
            pltpu.VMEM((SHIFTS * BOXES, TERMS * K, PLANE), BF16),
            pltpu.VMEM((HALVES, DEVICES, CAP, K, HALF), BF16),
            pltpu.VMEM((ITERS, HALVES, DEVICES, CAP, K, HALF), BF16),
            pltpu.VMEM((GROUP, K, PLANE), BF16),
            pltpu.VMEM((ITERS, GROUP, K, PLANE), BF16),
            pltpu.VMEM((GROUP, K, PLANE), BF16),
            pltpu.VMEM((ITERS, GROUP, K, PLANE), BF16),
            pltpu.VMEM((DEVICES, 1, PLANE), I32),
            pltpu.VMEM((8, *mat), BF16),
            pltpu.VMEM((4, *mat), BF16),
            pltpu.VMEM((4, *mat), BF16),
            pltpu.VMEM((3, *mat), BF16),
            pltpu.VMEM((BOXES, K, PLANE), BF16),
            pltpu.VMEM((BOXES, K, PLANE), BF16),
            pltpu.VMEM((3, K, TERMS * K), BF16),
            dma((TERMS,)),
            dma((2,)),
            dma((ITERS,)),
            dma((ITERS, HALVES, BURSTS)),
            dma((ITERS, 4)),
        ],
        compiler_params=pltpu.CompilerParams(
            vmem_limit_bytes=VMEM_LIMIT, collective_id=0, has_side_effects=True
        ),
    )(slots, labels, coefficients, potential, to_values, two_scale, octant, xk, yz_kernels)


def solution(mesh):
    spread = P(("oct", "sub"), None)
    placed = (spread, spread, P(), P(), P(), P(), spread, spread, P(("oct", "sub")), P(("oct", "sub")))
    return jax.shard_map(
        shards, mesh=mesh, in_specs=placed, out_specs=(spread, spread), check_vma=False
    )
```

```python
import functools

import jax
import jax.numpy as jnp
from jax import lax
from jax.experimental import pallas as pl
from jax.experimental.pallas import tpu as pltpu
from jax.sharding import PartitionSpec as P

F32, BF16, I32 = jnp.float32, jnp.bfloat16, jnp.int32
MESH = pl.DeviceIdType.MESH
ITERS = 2
K = 16
PLANE = K * K
BOXES = 16
ROWS = BOXES * K
TERMS = 20
SHIFTS = 9
LIST = 16
DEVICES = 128
GROUP = 64
CAP = 2
HALVES, HALF = 2, PLANE // 2
SLOTS = DEVICES * CAP
WIDE = SHIFTS * PLANE
SIDE = 4
BURSTS = GROUP // SIDE
BATCH = DEVICES // BURSTS
UP_BATCH = 16
NO_PARENT = 2
CHILD, HOME, TABLE = 2 * SLOTS, 2 * SLOTS + DEVICES, 2 * SLOTS + 2 * DEVICES
VMEM_LIMIT = 67_000_000


def mm(a, b):
    return jnp.dot(a, b, preferred_element_type=F32)


def split(a):
    hi = a.astype(BF16)
    return hi, (a - hi.astype(F32)).astype(BF16)


def mm3(a, b):
    return mm(a[0], b[0]) + (mm(a[0], b[1]) + mm(a[1], b[0]))


def exact(a, b):
    return jnp.dot(a, b, precision=lax.Precision.HIGHEST, preferred_element_type=F32)


def iotas(shape):
    return lax.broadcasted_iota(I32, shape, 0), lax.broadcasted_iota(I32, shape, 1)


def spreads():
    row, col = iotas((ROWS, K))
    high, low = (row // K == col).astype(F32), (row % K == col).astype(F32)
    row, col = iotas((K, ROWS))
    high_t, low_t = (col // K == row).astype(F32), (col % K == row).astype(F32)
    return high, low, high_t, low_t


def fill_values(table, mats):
    high, low, high_t, low_t = spreads()
    row, col = iotas((ROWS, ROWS))
    table_t = table.T
    hh = exact(exact(high, table), high_t)
    ll = exact(exact(low, table), low_t)
    hh_t = exact(exact(high, table_t), high_t)
    ll_t = exact(exact(low, table_t), low_t)
    lh_t = exact(exact(low, table_t), high_t)
    left = jnp.where(row % K == col % K, hh, 0.0)
    left_back = jnp.where(row // K == col % K, lh_t, 0.0)
    for n, mat in enumerate((left, hh_t * ll_t, left_back, hh * ll)):
        hi, lo = split(mat)
        mats[2 * n] = hi
        mats[2 * n + 1] = lo


def octant_rows(octant_ref, digit):
    row, col = iotas((ROWS, BOXES))
    hit = (row // K if digit == "high" else row % K) == col
    return jnp.sum(jnp.where(hit, octant_ref[...], 0), axis=1, keepdims=True)


def fill_tree(scale_ref, octant_ref, up_mats, down_mats, sides):
    high, low, high_t, low_t = spreads()
    row, col = iotas((ROWS, ROWS))
    filters = [scale_ref[c] for c in range(2)]
    turned = [f.T for f in filters]
    for mats, pair in ((up_mats, turned), (down_mats, filters)):
        highs = [exact(exact(high, f), high_t) for f in pair]
        lows = [exact(exact(low, f), low_t) for f in pair]
        for c in range(4):
            mats[c] = (highs[c // 2] * lows[c % 2]).astype(BF16)
    ups = [exact(exact(low, f), low_t) for f in filters]
    up = jnp.where(octant_rows(octant_ref, "high") // 4 == 1, ups[1], ups[0])
    sides[0] = jnp.where(row // K == col // K, up, 0.0).astype(BF16)
    downs = [exact(exact(high, f), low_t) for f in turned]
    down = jnp.where(octant_rows(octant_ref, "low") // 4 == 1, downs[1], downs[0])
    same = row % K == col // K
    sides[1] = jnp.where(same, down, 0.0).astype(BF16)
    sides[2] = jnp.where(same & (row // K == col % K), 1.0, 0.0).astype(BF16)


def by_octant(blocks, octants, mats):
    out = mm(blocks, mats[0])
    for c in range(1, 4):
        out = jnp.where(octants == c, mm(blocks, mats[c]), out)
    return out


def source_of(current, pot_ref, mats):
    pairs = [(mats[2 * n], mats[2 * n + 1]) for n in range(4)]
    values = mm3(pairs[0], split(mm3(split(current), pairs[1])))
    product = values * (rows_of(pot_ref) + 0.25 * values * values)
    return mm3(pairs[2], split(mm3(split(product), pairs[3]))).astype(BF16)


def corrected(gathered, matched, octants, down_mats, sides):
    inner = by_octant(matched[...].reshape(ROWS, PLANE), octants, down_mats)
    g_hi, g_lo = split(gathered)
    return mm(sides[2], g_hi) + mm(sides[2], g_lo) - mm(sides[1], inner.astype(BF16))


def rows_of(ref):
    return jnp.concatenate([ref[:, x * PLANE : (x + 1) * PLANE] for x in range(K)], axis=0)


def place():
    sub = lax.axis_index("sub")
    return lax.axis_index("oct"), sub // (SIDE * SIDE), (sub // SIDE) % SIDE, sub % SIDE


def burst_of(n, sign):
    core, x, z, y = place()
    a, kz = n // SIDE, lax.rem(n, SIDE)
    z_part = lax.rem(z + sign * kz + SIDE, SIDE) * SIDE
    chips = []
    for ky in range(SIDE):
        x_part = lax.rem(x + sign * (a + kz + ky) + 3 * SIDE, SIDE) * (SIDE * SIDE)
        chips.append(x_part + z_part + lax.rem(y + sign * ky + SIDE, SIDE))
    cores = (core, 1 - core)
    return [[(cores[c], chips[t]) for c in range(2)] for t in range(SIDE)]


def in_bursts(ship, fill=None):
    if fill is None:
        ship(0, 1)

        def step(n, carry):
            ship(n, 0)
            return carry

        lax.fori_loop(1, BURSTS, step, 0)
        return
    fill(0)
    ship(0, 1)
    fill(1)

    def step(n, carry):
        ship(n - 1, 0)
        fill(n)
        return carry

    lax.fori_loop(2, BURSTS, step, 0)
    ship(BURSTS - 1, 0)


def displacement_order(own, core, sub):
    core_0, x, z, y = own
    kx, kz, ky = (sub // 16 - x) & 3, (sub // SIDE - z) & 3, (sub - y) & 3
    u = (((kx - kz - ky) & 3) * SIDE + kz) * SIDE + ky
    return 2 * u + ((core - core_0) & 1)


def whole(a):
    return (a + 1.5).astype(I32) - 1


def route_kernel(dest_ref, disp_ref, parent_ref, table_ref, labels_ref):
    own = place()
    high, low, high_t, low_t = spreads()
    count = BOXES * LIST

    def as_row(v):
        spread = exact(v.astype(F32), low_t)
        return whole(jnp.sum(jnp.where(high_t > 0.5, spread, 0.0), axis=0, keepdims=True))

    def as_col(v):
        spread = exact(high, v.astype(F32))
        return whole(jnp.sum(jnp.where(low > 0.5, spread, 0.0), axis=1, keepdims=True))

    row, col = iotas((count, count))

    def order_of(dest):
        block = dest >> 4
        order = displacement_order(own, block >> 6, block & (GROUP - 1))
        return jnp.where(dest >= 0, order, -1)

    dest_row, dest_col, disp_col = as_row(dest_ref[...]), as_col(dest_ref[...]), as_col(disp_ref[...])
    order_row, order_col = order_of(dest_row), order_of(dest_col)
    same = order_row == order_col
    rank_row = jnp.sum(jnp.where(same & (row < col), 1, 0), axis=0, keepdims=True)
    rank_col = jnp.sum(jnp.where(same & (col < row), 1, 0), axis=1, keepdims=True)
    at_row = jnp.where(order_row >= 0, order_row * CAP + rank_row, -1)
    at_col = jnp.where(order_col >= 0, order_col * CAP + rank_col, -1)
    along_x = (disp_col * 57) >> 9
    box_col = lax.broadcasted_iota(I32, (count, 1), 0) // LIST
    plane_col = (disp_col - SHIFTS * along_x) * BOXES + box_col
    hit = at_col == col
    table_ref[:, :SLOTS] = jnp.sum(jnp.where(hit, plane_col, 0), axis=0, keepdims=True)
    table_ref[:, SLOTS : 2 * SLOTS] = jnp.sum(jnp.where(hit, along_x, 0), axis=0, keepdims=True)

    parent_row = parent_ref[...] & (2 * GROUP - 1)
    up_row = displacement_order(own, own[0], parent_row >> 1)
    row_b, col_b = iotas((BOXES, BOXES))
    up_col = jnp.sum(jnp.where(row_b == col_b, up_row, 0), axis=1, keepdims=True)
    row_u, col_u = iotas((BOXES, DEVICES))
    children = jnp.sum(jnp.where(up_col == 2 * col_u, row_u, 0), axis=0, keepdims=True)
    table_ref[:, CHILD:HOME] = children
    table_ref[:, HOME : HOME + BOXES] = up_row >> 1

    order, lane = iotas((DEVICES, count))
    which = (dest_row & (BOXES - 1)) - BOXES
    labels = [
        jnp.sum(jnp.where(at_row == order * CAP + c, which, 0), axis=1, keepdims=True) + BOXES
        for c in range(CAP)
    ]
    order_b, lane_b = iotas((DEVICES, BOXES))
    ups = jnp.sum(
        jnp.where(up_row == order_b, (parent_row & 1) - NO_PARENT, 0), axis=1, keepdims=True
    )
    marks = jnp.where((lane // K) % CAP == 0, labels[0], labels[1]) + 32 * (ups + NO_PARENT)
    labels_ref[...] = marks.reshape(DEVICES, 1, PLANE)


def main_kernel(
    slots_ref, labels_ref, coef_ref, pot_ref, table_ref, scale_ref, octant_ref, xk_ref, yz_hbm,
    gathered_ref, matched, sums_ref, down_mats, sides,
    yz_buf, partial, send, recv, up_send, up_recv, down_send, down_recv, tags,
    mats, up_mats, lifted, xk,
    yz_sem, tag_sem, send_sem, recv_sem, tree_sem,
):
    for m in range(TERMS):
        pltpu.make_async_copy(
            yz_hbm.at[:, m * WIDE : (m + 1) * WIDE], yz_buf.at[m], yz_sem.at[m]
        ).start()
    barrier = pltpu.get_barrier_semaphore()
    someone = burst_of(jnp.int32(0), 1)[1][0]

    def greet(n, skip):
        devices = burst_of(jnp.int32(n), 1)
        for e in range(skip, BATCH):
            pl.semaphore_signal(
                barrier, inc=1, device_id=devices[e // 2][e % 2], device_id_type=MESH
            )

    in_bursts(greet)

    def remote(source, target, out_sem, in_sem, device):
        return pltpu.make_async_remote_copy(
            src_ref=source, dst_ref=target, send_sem=out_sem, recv_sem=in_sem,
            device_id=device, device_id_type=MESH,
        )

    def arrived(region, out_sem, in_sem):
        remote(region, region, out_sem, in_sem, someone).wait_recv()

    def left(region, out_sem, in_sem):
        remote(region, region, out_sem, in_sem, someone).wait_send()

    xk[...] = xk_ref[...].astype(F32).T.astype(BF16).reshape(3, K, TERMS * K)
    fill_values(table_ref[...], mats)
    source = source_of(rows_of(coef_ref), pot_ref, mats)
    octants = octant_rows(octant_ref, "high") % 4
    row, col = iotas((ROWS, ROWS))
    same_plane = row % K == col % K
    row_box = row // K

    pl.semaphore_wait(barrier, DEVICES - 1)

    def tell(n, skip):
        devices = burst_of(jnp.int32(n), 1)
        for e in range(skip, BATCH):
            j = n * BATCH + e
            remote(
                labels_ref.at[j], tags.at[j], tag_sem.at[0], tag_sem.at[1], devices[e // 2][e % 2]
            ).start()

    tell(0, 1)
    tags[0] = labels_ref[0]

    for it in range(ITERS):

        if it > 0:
            left(send.at[:, pl.ds(1, DEVICES - 1)], send_sem.at[it - 1], recv_sem.at[0, 0, 0])
        for h in range(HALVES):
            lanes = slice(h * HALF, (h + 1) * HALF)

            def product(pair, it=it, source=source, h=h, lanes=lanes):
                if it == 0 and h == 0:
                    for e in range(2):
                        m = 2 * pair + e
                        pltpu.make_async_copy(
                            yz_hbm.at[:, pl.ds(0, WIDE)], yz_buf.at[m], yz_sem.at[m]
                        ).wait()
                at = pl.multiple_of(pair * 2 * K, 2 * K)
                for p in range(SHIFTS):
                    lo = p * PLANE + h * HALF
                    both = jnp.concatenate(
                        [yz_buf[2 * pair + e, :, lo : lo + HALF] for e in range(2)], axis=1
                    )
                    part = mm(source, both).astype(BF16)
                    for e in range(2):
                        partial[p * BOXES : (p + 1) * BOXES, pl.ds(at + e * K, K), lanes] = part[
                            :, e * HALF : (e + 1) * HALF
                        ].reshape(BOXES, K, HALF)

            def step(pair, carry, product=product):
                product(pair)
                return carry

            def telling(pair, carry, product=product):
                for e in range(3):
                    tell(1 + 3 * pair + e, 0)
                product(pair)
                return carry

            if it == 0 and h == 0:
                lax.fori_loop(0, BURSTS // 3, telling, 0)
                lax.fori_loop(BURSTS // 3, TERMS // 2, step, 0)
            else:
                lax.fori_loop(0, TERMS // 2, step, 0)

            def ship(n, skip, it=it, h=h):
                devices = burst_of(jnp.int32(n), 1)
                for e in range(skip, BATCH):
                    j = n * BATCH + e
                    remote(
                        send.at[h, j], recv.at[it, h, j], send_sem.at[it], recv_sem.at[it, h, n],
                        devices[e // 2][e % 2],
                    ).start()

            def fill(n, h=h, lanes=lanes):
                for e in range(BATCH):
                    j = n * BATCH + e
                    at = [j * CAP + c for c in range(CAP)]
                    factors = jnp.concatenate([xk[slots_ref[0, SLOTS + i]] for i in at], axis=0)
                    parts = jnp.concatenate([partial[slots_ref[0, i], :, lanes] for i in at], axis=1)
                    both = mm(factors, parts).astype(BF16)
                    for c in range(CAP):
                        send[h, j, c] = both[c * K : (c + 1) * K, c * HALF : (c + 1) * HALF]

            in_bursts(ship, fill)
            recv[it, h, 0] = send[h, 0]

        if it == 0:
            fill_tree(scale_ref, octant_ref, up_mats, down_mats, sides)
        if it == 0:
            arrived(tags.at[pl.ds(1, DEVICES - 1)], tag_sem.at[0], tag_sem.at[1])

        halves = []
        for h in range(HALVES):
            total = jnp.zeros((ROWS, HALF), F32)
            for g in range(BURSTS):
                lo = max(1, g * BATCH)
                arrived(
                    recv.at[it, h, pl.ds(lo, (g + 1) * BATCH - lo)],
                    send_sem.at[it], recv_sem.at[it, h, g],
                )
                marks = tags[g * BATCH : (g + 1) * BATCH].reshape(BATCH, PLANE) % 32
                row8, col8 = iotas((BATCH, PLANE))
                marks = jnp.sum(
                    jnp.where(row8 == col8 // (CAP * K), marks, 0), axis=0, keepdims=True
                )
                member = jnp.where(same_plane & (marks == row_box), 1.0, 0.0).astype(BF16)
                block = recv[it, h, g * BATCH : (g + 1) * BATCH].reshape(ROWS, HALF)
                total = total + mm(member, block)
            halves.append(total)
        gathered = jnp.concatenate(halves, axis=1)

        inner = by_octant(gathered.astype(BF16), octants, up_mats)
        up = mm(sides[0], inner.astype(BF16))
        lifted[...] = up.astype(BF16).reshape(BOXES, K, PLANE)

        if it > 0:
            left(up_send.at[pl.ds(1, GROUP - 1)], tree_sem.at[it - 1, 0], tree_sem.at[0, 1])

        def ship_up(n, skip, it=it):
            devices = burst_of(jnp.int32(n), 1)
            for t in range(skip, SIDE):
                u = n * SIDE + t
                remote(
                    up_send.at[u], up_recv.at[it, u], tree_sem.at[it, 0], tree_sem.at[it, 1],
                    devices[t][0],
                ).start()

        def fill_up(n):
            for t in range(SIDE):
                up_send[n * SIDE + t] = lifted[slots_ref[0, CHILD + n * SIDE + t]]

        in_bursts(ship_up, fill_up)
        up_recv[it, 0] = up_send[0]
        arrived(up_recv.at[it, pl.ds(1, GROUP - 1)], tree_sem.at[it, 0], tree_sem.at[it, 1])

        sums = jnp.zeros((2 * K, PLANE), F32)
        row_p, col_p = iotas((2 * K, PLANE))
        for h in range(GROUP // UP_BATCH):
            span = 2 * UP_BATCH
            marks = tags[h * span : (h + 1) * span].reshape(span, PLANE) // 32
            row_s, col_s = iotas((span, PLANE))
            marks = jnp.sum(jnp.where(row_s == 2 * (col_s // K), marks, 0), axis=0, keepdims=True)
            member = jnp.where((row_p % K == col_p % K) & (marks == row_p // K), 1.0, 0.0)
            block = up_recv[it, h * UP_BATCH : (h + 1) * UP_BATCH].reshape(ROWS, PLANE)
            sums = sums + mm(member.astype(BF16), block)
        if it == ITERS - 1:
            sums_ref[...] = sums
            gathered_ref[...] = gathered

        if it > 0:
            left(down_send.at[pl.ds(1, GROUP - 1)], tree_sem.at[it - 1, 2], tree_sem.at[0, 3])

        def ship_down(n, skip, it=it):
            devices = burst_of(jnp.int32(n), -1)
            for t in range(skip, SIDE):
                u = n * SIDE + t
                remote(
                    down_send.at[u], down_recv.at[it, u], tree_sem.at[it, 2], tree_sem.at[it, 3],
                    devices[t][0],
                ).start()

        def fill_down(n, sums=sums):
            for t in range(SIDE):
                second = tags[2 * (n * SIDE + t)] // 32 == 1
                down_send[n * SIDE + t] = jnp.where(second, sums[K:], sums[:K]).astype(BF16)

        in_bursts(ship_down, fill_down)
        down_recv[it, 0] = down_send[0]
        arrived(down_recv.at[it, pl.ds(1, GROUP - 1)], tree_sem.at[it, 2], tree_sem.at[it, 3])

        for b in range(BOXES):
            matched[b] = down_recv[it, slots_ref[0, HOME + b]]
        if it < ITERS - 1:
            current = corrected(gathered, matched, octants, down_mats, sides)
            source = source_of(current, pot_ref, mats)

    last = ITERS - 1
    left(tags.at[pl.ds(1, DEVICES - 1)], tag_sem.at[0], tag_sem.at[1])
    left(send.at[:, pl.ds(1, DEVICES - 1)], send_sem.at[last], recv_sem.at[0, 0, 0])
    left(up_send.at[pl.ds(1, GROUP - 1)], tree_sem.at[last, 0], tree_sem.at[0, 1])
    left(down_send.at[pl.ds(1, GROUP - 1)], tree_sem.at[last, 2], tree_sem.at[0, 3])


def last_kernel(gathered_ref, matched, sums_ref, down_mats, sides, octant_ref, field_ref, parents_ref):
    octants = octant_rows(octant_ref, "high") % 4
    current = corrected(gathered_ref[...], matched, octants, down_mats, sides)
    for x in range(K):
        field_ref[:, x * PLANE : (x + 1) * PLANE] = current[x * BOXES : (x + 1) * BOXES, :]
    for p in range(2):
        for i in range(K):
            at = p * K + i
            parents_ref[p : p + 1, i * PLANE : (i + 1) * PLANE] = sums_ref[at : at + 1, :]


SMEM = pl.BlockSpec(memory_space=pltpu.SMEM)
VMEM = pl.BlockSpec(memory_space=pltpu.VMEM)
ANY = pl.BlockSpec(memory_space=pl.ANY)


def shards(
    coefficients,
    potential,
    to_values,
    x_kernels,
    yz_kernels,
    two_scale,
    disp_ids,
    dest_box,
    parent_of,
    child_octant,
):
    xk = x_kernels.transpose(0, 2, 1).reshape(TERMS * K, 3 * K)
    octant = child_octant.reshape(1, BOXES)
    ints = functools.partial(jax.ShapeDtypeStruct, dtype=I32)
    slots, labels = pl.pallas_call(
        route_kernel,
        out_shape=(ints((1, TABLE)), ints((DEVICES, 1, PLANE))),
        in_specs=[VMEM] * 3,
        out_specs=(VMEM, VMEM),
    )(dest_box, disp_ids, parent_of.reshape(1, BOXES))
    mat = (ROWS, ROWS)
    dma = pltpu.SemaphoreType.DMA
    shape = jax.ShapeDtypeStruct
    parts = pl.pallas_call(
        main_kernel,
        out_shape=(
            shape(mat, F32),
            shape((BOXES, K, PLANE), BF16),
            shape((2 * K, PLANE), F32),
            shape((4, *mat), BF16),
            shape((3, *mat), BF16),
        ),
        in_specs=[SMEM] + [VMEM] * 7 + [ANY],
        out_specs=(VMEM,) * 5,
        scratch_shapes=[
            pltpu.VMEM((TERMS, PLANE, WIDE), BF16),
            pltpu.VMEM((SHIFTS * BOXES, TERMS * K, PLANE), BF16),
            pltpu.VMEM((HALVES, DEVICES, CAP, K, HALF), BF16),
            pltpu.VMEM((ITERS, HALVES, DEVICES, CAP, K, HALF), BF16),
            pltpu.VMEM((GROUP, K, PLANE), BF16),
            pltpu.VMEM((ITERS, GROUP, K, PLANE), BF16),
            pltpu.VMEM((GROUP, K, PLANE), BF16),
            pltpu.VMEM((ITERS, GROUP, K, PLANE), BF16),
            pltpu.VMEM((DEVICES, 1, PLANE), I32),
            pltpu.VMEM((8, *mat), BF16),
            pltpu.VMEM((4, *mat), BF16),
            pltpu.VMEM((BOXES, K, PLANE), BF16),
            pltpu.VMEM((3, K, TERMS * K), BF16),
            dma((TERMS,)),
            dma((2,)),
            dma((ITERS,)),
            dma((ITERS, HALVES, BURSTS)),
            dma((ITERS, 4)),
        ],
        compiler_params=pltpu.CompilerParams(
            vmem_limit_bytes=VMEM_LIMIT, collective_id=0, has_side_effects=True
        ),
    )(slots, labels, coefficients, potential, to_values, two_scale, octant, xk, yz_kernels)
    return pl.pallas_call(
        last_kernel,
        out_shape=(shape((BOXES, K * PLANE), F32), shape((2, K * PLANE), F32)),
        in_specs=[VMEM] * 6,
        out_specs=(VMEM, VMEM),
    )(*parts, octant)


def solution(mesh):
    spread = P(("oct", "sub"), None)
    placed = (spread, spread, P(), P(), P(), P(), spread, spread, P(("oct", "sub")), P(("oct", "sub")))
    return jax.shard_map(
        shards, mesh=mesh, in_specs=placed, out_specs=(spread, spread), check_vma=False
    )
```

```python
import functools

import jax
import jax.numpy as jnp
from jax import lax
from jax.experimental import pallas as pl
from jax.experimental.pallas import tpu as pltpu
from jax.sharding import PartitionSpec as P

F32, BF16, I32 = jnp.float32, jnp.bfloat16, jnp.int32
MESH = pl.DeviceIdType.MESH
ITERS = 2
K = 16
PLANE = K * K
BOXES = 16
ROWS = BOXES * K
TERMS = 20
SHIFTS = 9
LIST = 16
DEVICES = 128
GROUP = 64
CAP = 2
HALVES, HALF = 2, PLANE // 2
SLOTS = DEVICES * CAP
WIDE = SHIFTS * PLANE
SIDE = 4
BURSTS = GROUP // SIDE
BATCH = DEVICES // BURSTS
UP_BATCH = 16
NO_PARENT = 2
CHILD, HOME, TABLE = 2 * SLOTS, 2 * SLOTS + DEVICES, 2 * SLOTS + 2 * DEVICES
VMEM_LIMIT = 67_000_000


def mm(a, b):
    return jnp.dot(a, b, preferred_element_type=F32)


def split(a):
    hi = a.astype(BF16)
    return hi, (a - hi.astype(F32)).astype(BF16)


def mm3(a, b):
    return mm(a[0], b[0]) + (mm(a[0], b[1]) + mm(a[1], b[0]))


def exact(a, b):
    return jnp.dot(a, b, precision=lax.Precision.HIGHEST, preferred_element_type=F32)


def iotas(shape):
    return lax.broadcasted_iota(I32, shape, 0), lax.broadcasted_iota(I32, shape, 1)


def spreads():
    row, col = iotas((ROWS, K))
    high, low = (row // K == col).astype(F32), (row % K == col).astype(F32)
    row, col = iotas((K, ROWS))
    high_t, low_t = (col // K == row).astype(F32), (col % K == row).astype(F32)
    return high, low, high_t, low_t


def fill_values(table, mats):
    high, low, high_t, low_t = spreads()
    row, col = iotas((ROWS, ROWS))
    table_t = table.T
    hh = exact(exact(high, table), high_t)
    ll = exact(exact(low, table), low_t)
    hh_t = exact(exact(high, table_t), high_t)
    ll_t = exact(exact(low, table_t), low_t)
    lh_t = exact(exact(low, table_t), high_t)
    left = jnp.where(row % K == col % K, hh, 0.0)
    left_back = jnp.where(row // K == col % K, lh_t, 0.0)
    for n, mat in enumerate((left, hh_t * ll_t, left_back, hh * ll)):
        hi, lo = split(mat)
        mats[2 * n] = hi
        mats[2 * n + 1] = lo


def octant_rows(octant_ref, digit):
    row, col = iotas((ROWS, BOXES))
    hit = (row // K if digit == "high" else row % K) == col
    return jnp.sum(jnp.where(hit, octant_ref[...], 0), axis=1, keepdims=True)


def fill_tree(scale_ref, octant_ref, up_mats, down_mats, sides):
    high, low, high_t, low_t = spreads()
    row, col = iotas((ROWS, ROWS))
    filters = [scale_ref[c] for c in range(2)]
    turned = [f.T for f in filters]
    for mats, pair in ((up_mats, turned), (down_mats, filters)):
        highs = [exact(exact(high, f), high_t) for f in pair]
        lows = [exact(exact(low, f), low_t) for f in pair]
        for c in range(4):
            mats[c] = (highs[c // 2] * lows[c % 2]).astype(BF16)
    ups = [exact(exact(low, f), low_t) for f in filters]
    up = jnp.where(octant_rows(octant_ref, "high") // 4 == 1, ups[1], ups[0])
    sides[0] = jnp.where(row // K == col // K, up, 0.0).astype(BF16)
    downs = [exact(exact(high, f), low_t) for f in turned]
    down = jnp.where(octant_rows(octant_ref, "low") // 4 == 1, downs[1], downs[0])
    same = row % K == col // K
    sides[1] = jnp.where(same, down, 0.0).astype(BF16)
    sides[2] = jnp.where(same & (row // K == col % K), 1.0, 0.0).astype(BF16)


def by_octant(blocks, octants, mats):
    out = mm(blocks, mats[0])
    for c in range(1, 4):
        out = jnp.where(octants == c, mm(blocks, mats[c]), out)
    return out


def source_of(current, pot_ref, mats):
    pairs = [(mats[2 * n], mats[2 * n + 1]) for n in range(2)]
    values = mm3(pairs[0], split(mm3(split(current), pairs[1])))
    product = values * (rows_of(pot_ref) + 0.25 * values * values)
    return mm(mats[2 * 2], mm(product.astype(BF16), mats[2 * 3]).astype(BF16)).astype(BF16)


def corrected(gathered, matched, octants, down_mats, sides):
    inner = by_octant(matched[...].reshape(ROWS, PLANE), octants, down_mats)
    g_hi, g_lo = split(gathered)
    return mm(sides[2], g_hi) + mm(sides[2], g_lo) - mm(sides[1], inner.astype(BF16))


def rows_of(ref):
    return jnp.concatenate([ref[:, x * PLANE : (x + 1) * PLANE] for x in range(K)], axis=0)


def place():
    sub = lax.axis_index("sub")
    return lax.axis_index("oct"), sub // (SIDE * SIDE), (sub // SIDE) % SIDE, sub % SIDE


def burst_of(n, sign):
    core, x, z, y = place()
    a, kz = n // SIDE, lax.rem(n, SIDE)
    z_part = lax.rem(z + sign * kz + SIDE, SIDE) * SIDE
    chips = []
    for ky in range(SIDE):
        x_part = lax.rem(x + sign * (a + kz + ky) + 3 * SIDE, SIDE) * (SIDE * SIDE)
        chips.append(x_part + z_part + lax.rem(y + sign * ky + SIDE, SIDE))
    cores = (core, 1 - core)
    return [[(cores[c], chips[t]) for c in range(2)] for t in range(SIDE)]


def in_bursts(ship, fill=None):
    if fill is None:
        ship(0, 1)

        def step(n, carry):
            ship(n, 0)
            return carry

        lax.fori_loop(1, BURSTS, step, 0)
        return
    fill(0)
    ship(0, 1)
    fill(1)

    def step(n, carry):
        ship(n - 1, 0)
        fill(n)
        return carry

    lax.fori_loop(2, BURSTS, step, 0)
    ship(BURSTS - 1, 0)


def displacement_order(own, core, sub):
    core_0, x, z, y = own
    kx, kz, ky = (sub // 16 - x) & 3, (sub // SIDE - z) & 3, (sub - y) & 3
    u = (((kx - kz - ky) & 3) * SIDE + kz) * SIDE + ky
    return 2 * u + ((core - core_0) & 1)


def whole(a):
    return (a + 1.5).astype(I32) - 1


def route_kernel(dest_ref, disp_ref, parent_ref, table_ref, labels_ref):
    own = place()
    high, low, high_t, low_t = spreads()
    count = BOXES * LIST

    def as_row(v):
        spread = exact(v.astype(F32), low_t)
        return whole(jnp.sum(jnp.where(high_t > 0.5, spread, 0.0), axis=0, keepdims=True))

    def as_col(v):
        spread = exact(high, v.astype(F32))
        return whole(jnp.sum(jnp.where(low > 0.5, spread, 0.0), axis=1, keepdims=True))

    row, col = iotas((count, count))

    def order_of(dest):
        block = dest >> 4
        order = displacement_order(own, block >> 6, block & (GROUP - 1))
        return jnp.where(dest >= 0, order, -1)

    dest_row, dest_col, disp_col = as_row(dest_ref[...]), as_col(dest_ref[...]), as_col(disp_ref[...])
    order_row, order_col = order_of(dest_row), order_of(dest_col)
    same = order_row == order_col
    rank_row = jnp.sum(jnp.where(same & (row < col), 1, 0), axis=0, keepdims=True)
    rank_col = jnp.sum(jnp.where(same & (col < row), 1, 0), axis=1, keepdims=True)
    at_row = jnp.where(order_row >= 0, order_row * CAP + rank_row, -1)
    at_col = jnp.where(order_col >= 0, order_col * CAP + rank_col, -1)
    along_x = (disp_col * 57) >> 9
    box_col = lax.broadcasted_iota(I32, (count, 1), 0) // LIST
    plane_col = (disp_col - SHIFTS * along_x) * BOXES + box_col
    hit = at_col == col
    table_ref[:, :SLOTS] = jnp.sum(jnp.where(hit, plane_col, 0), axis=0, keepdims=True)
    table_ref[:, SLOTS : 2 * SLOTS] = jnp.sum(jnp.where(hit, along_x, 0), axis=0, keepdims=True)

    parent_row = parent_ref[...] & (2 * GROUP - 1)
    up_row = displacement_order(own, own[0], parent_row >> 1)
    row_b, col_b = iotas((BOXES, BOXES))
    up_col = jnp.sum(jnp.where(row_b == col_b, up_row, 0), axis=1, keepdims=True)
    row_u, col_u = iotas((BOXES, DEVICES))
    children = jnp.sum(jnp.where(up_col == 2 * col_u, row_u, 0), axis=0, keepdims=True)
    table_ref[:, CHILD:HOME] = children
    table_ref[:, HOME : HOME + BOXES] = up_row >> 1

    order, lane = iotas((DEVICES, count))
    which = (dest_row & (BOXES - 1)) - BOXES
    labels = [
        jnp.sum(jnp.where(at_row == order * CAP + c, which, 0), axis=1, keepdims=True) + BOXES
        for c in range(CAP)
    ]
    order_b, lane_b = iotas((DEVICES, BOXES))
    ups = jnp.sum(
        jnp.where(up_row == order_b, (parent_row & 1) - NO_PARENT, 0), axis=1, keepdims=True
    )
    marks = jnp.where((lane // K) % CAP == 0, labels[0], labels[1]) + 32 * (ups + NO_PARENT)
    labels_ref[...] = marks.reshape(DEVICES, 1, PLANE)


def main_kernel(
    slots_ref, labels_ref, coef_ref, pot_ref, table_ref, scale_ref, octant_ref, xk_ref, yz_hbm,
    gathered_ref, matched, sums_ref, down_mats, sides,
    yz_buf, partial, send, recv, up_send, up_recv, down_send, down_recv, tags,
    mats, up_mats, lifted, xk,
    yz_sem, tag_sem, send_sem, recv_sem, tree_sem,
):
    for m in range(TERMS):
        pltpu.make_async_copy(
            yz_hbm.at[:, m * WIDE : (m + 1) * WIDE], yz_buf.at[m], yz_sem.at[m]
        ).start()
    barrier = pltpu.get_barrier_semaphore()
    someone = burst_of(jnp.int32(0), 1)[1][0]

    def greet(n, skip):
        devices = burst_of(jnp.int32(n), 1)
        for e in range(skip, BATCH):
            pl.semaphore_signal(
                barrier, inc=1, device_id=devices[e // 2][e % 2], device_id_type=MESH
            )

    in_bursts(greet)

    def remote(source, target, out_sem, in_sem, device):
        return pltpu.make_async_remote_copy(
            src_ref=source, dst_ref=target, send_sem=out_sem, recv_sem=in_sem,
            device_id=device, device_id_type=MESH,
        )

    def arrived(region, out_sem, in_sem):
        remote(region, region, out_sem, in_sem, someone).wait_recv()

    def left(region, out_sem, in_sem):
        remote(region, region, out_sem, in_sem, someone).wait_send()

    xk[...] = xk_ref[...].astype(F32).T.astype(BF16).reshape(3, K, TERMS * K)
    fill_values(table_ref[...], mats)
    source = source_of(rows_of(coef_ref), pot_ref, mats)
    octants = octant_rows(octant_ref, "high") % 4
    row, col = iotas((ROWS, ROWS))
    same_plane = row % K == col % K
    row_box = row // K

    pl.semaphore_wait(barrier, DEVICES - 1)

    def tell(n, skip):
        devices = burst_of(jnp.int32(n), 1)
        for e in range(skip, BATCH):
            j = n * BATCH + e
            remote(
                labels_ref.at[j], tags.at[j], tag_sem.at[0], tag_sem.at[1], devices[e // 2][e % 2]
            ).start()

    tell(0, 1)
    tags[0] = labels_ref[0]

    for it in range(ITERS):

        if it > 0:
            left(send.at[:, pl.ds(1, DEVICES - 1)], send_sem.at[it - 1], recv_sem.at[0, 0, 0])
        for h in range(HALVES):
            lanes = slice(h * HALF, (h + 1) * HALF)

            def product(pair, it=it, source=source, h=h, lanes=lanes):
                if it == 0 and h == 0:
                    for e in range(2):
                        m = 2 * pair + e
                        pltpu.make_async_copy(
                            yz_hbm.at[:, pl.ds(0, WIDE)], yz_buf.at[m], yz_sem.at[m]
                        ).wait()
                at = pl.multiple_of(pair * 2 * K, 2 * K)
                for p in range(SHIFTS):
                    lo = p * PLANE + h * HALF
                    both = jnp.concatenate(
                        [yz_buf[2 * pair + e, :, lo : lo + HALF] for e in range(2)], axis=1
                    )
                    part = mm(source, both).astype(BF16)
                    for e in range(2):
                        partial[p * BOXES : (p + 1) * BOXES, pl.ds(at + e * K, K), lanes] = part[
                            :, e * HALF : (e + 1) * HALF
                        ].reshape(BOXES, K, HALF)

            def step(pair, carry, product=product):
                product(pair)
                return carry

            def telling(pair, carry, product=product):
                for e in range(3):
                    tell(1 + 3 * pair + e, 0)
                product(pair)
                return carry

            if it == 0 and h == 0:
                lax.fori_loop(0, BURSTS // 3, telling, 0)
                lax.fori_loop(BURSTS // 3, TERMS // 2, step, 0)
            else:
                lax.fori_loop(0, TERMS // 2, step, 0)

            def ship(n, skip, it=it, h=h):
                devices = burst_of(jnp.int32(n), 1)
                for e in range(skip, BATCH):
                    j = n * BATCH + e
                    remote(
                        send.at[h, j], recv.at[it, h, j], send_sem.at[it], recv_sem.at[it, h, n],
                        devices[e // 2][e % 2],
                    ).start()

            def fill(n, h=h, lanes=lanes):
                for e in range(BATCH):
                    j = n * BATCH + e
                    at = [j * CAP + c for c in range(CAP)]
                    factors = jnp.concatenate([xk[slots_ref[0, SLOTS + i]] for i in at], axis=0)
                    parts = jnp.concatenate([partial[slots_ref[0, i], :, lanes] for i in at], axis=1)
                    both = mm(factors, parts).astype(BF16)
                    for c in range(CAP):
                        send[h, j, c] = both[c * K : (c + 1) * K, c * HALF : (c + 1) * HALF]

            in_bursts(ship, fill)
            recv[it, h, 0] = send[h, 0]

        if it == 0:
            fill_tree(scale_ref, octant_ref, up_mats, down_mats, sides)
        if it == 0:
            arrived(tags.at[pl.ds(1, DEVICES - 1)], tag_sem.at[0], tag_sem.at[1])

        halves = []
        for h in range(HALVES):
            total = jnp.zeros((ROWS, HALF), F32)
            for g in range(BURSTS):
                lo = max(1, g * BATCH)
                arrived(
                    recv.at[it, h, pl.ds(lo, (g + 1) * BATCH - lo)],
                    send_sem.at[it], recv_sem.at[it, h, g],
                )
                marks = tags[g * BATCH : (g + 1) * BATCH].reshape(BATCH, PLANE) % 32
                row8, col8 = iotas((BATCH, PLANE))
                marks = jnp.sum(
                    jnp.where(row8 == col8 // (CAP * K), marks, 0), axis=0, keepdims=True
                )
                member = jnp.where(same_plane & (marks == row_box), 1.0, 0.0).astype(BF16)
                block = recv[it, h, g * BATCH : (g + 1) * BATCH].reshape(ROWS, HALF)
                total = total + mm(member, block)
            halves.append(total)
        gathered = jnp.concatenate(halves, axis=1)

        inner = by_octant(gathered.astype(BF16), octants, up_mats)
        up = mm(sides[0], inner.astype(BF16))
        lifted[...] = up.astype(BF16).reshape(BOXES, K, PLANE)

        if it > 0:
            left(up_send.at[pl.ds(1, GROUP - 1)], tree_sem.at[it - 1, 0], tree_sem.at[0, 1])

        def ship_up(n, skip, it=it):
            devices = burst_of(jnp.int32(n), 1)
            for t in range(skip, SIDE):
                u = n * SIDE + t
                remote(
                    up_send.at[u], up_recv.at[it, u], tree_sem.at[it, 0], tree_sem.at[it, 1],
                    devices[t][0],
                ).start()

        def fill_up(n):
            for t in range(SIDE):
                up_send[n * SIDE + t] = lifted[slots_ref[0, CHILD + n * SIDE + t]]

        in_bursts(ship_up, fill_up)
        up_recv[it, 0] = up_send[0]
        arrived(up_recv.at[it, pl.ds(1, GROUP - 1)], tree_sem.at[it, 0], tree_sem.at[it, 1])

        sums = jnp.zeros((2 * K, PLANE), F32)
        row_p, col_p = iotas((2 * K, PLANE))
        for h in range(GROUP // UP_BATCH):
            span = 2 * UP_BATCH
            marks = tags[h * span : (h + 1) * span].reshape(span, PLANE) // 32
            row_s, col_s = iotas((span, PLANE))
            marks = jnp.sum(jnp.where(row_s == 2 * (col_s // K), marks, 0), axis=0, keepdims=True)
            member = jnp.where((row_p % K == col_p % K) & (marks == row_p // K), 1.0, 0.0)
            block = up_recv[it, h * UP_BATCH : (h + 1) * UP_BATCH].reshape(ROWS, PLANE)
            sums = sums + mm(member.astype(BF16), block)
        if it == ITERS - 1:
            sums_ref[...] = sums
            gathered_ref[...] = gathered

        if it > 0:
            left(down_send.at[pl.ds(1, GROUP - 1)], tree_sem.at[it - 1, 2], tree_sem.at[0, 3])

        def ship_down(n, skip, it=it):
            devices = burst_of(jnp.int32(n), -1)
            for t in range(skip, SIDE):
                u = n * SIDE + t
                remote(
                    down_send.at[u], down_recv.at[it, u], tree_sem.at[it, 2], tree_sem.at[it, 3],
                    devices[t][0],
                ).start()

        def fill_down(n, sums=sums):
            for t in range(SIDE):
                second = tags[2 * (n * SIDE + t)] // 32 == 1
                down_send[n * SIDE + t] = jnp.where(second, sums[K:], sums[:K]).astype(BF16)

        in_bursts(ship_down, fill_down)
        down_recv[it, 0] = down_send[0]
        arrived(down_recv.at[it, pl.ds(1, GROUP - 1)], tree_sem.at[it, 2], tree_sem.at[it, 3])

        for b in range(BOXES):
            matched[b] = down_recv[it, slots_ref[0, HOME + b]]
        if it < ITERS - 1:
            current = corrected(gathered, matched, octants, down_mats, sides)
            source = source_of(current, pot_ref, mats)

    last = ITERS - 1
    left(tags.at[pl.ds(1, DEVICES - 1)], tag_sem.at[0], tag_sem.at[1])
    left(send.at[:, pl.ds(1, DEVICES - 1)], send_sem.at[last], recv_sem.at[0, 0, 0])
    left(up_send.at[pl.ds(1, GROUP - 1)], tree_sem.at[last, 0], tree_sem.at[0, 1])
    left(down_send.at[pl.ds(1, GROUP - 1)], tree_sem.at[last, 2], tree_sem.at[0, 3])


def last_kernel(gathered_ref, matched, sums_ref, down_mats, sides, octant_ref, field_ref, parents_ref):
    octants = octant_rows(octant_ref, "high") % 4
    current = corrected(gathered_ref[...], matched, octants, down_mats, sides)
    for x in range(K):
        field_ref[:, x * PLANE : (x + 1) * PLANE] = current[x * BOXES : (x + 1) * BOXES, :]
    for p in range(2):
        for i in range(K):
            at = p * K + i
            parents_ref[p : p + 1, i * PLANE : (i + 1) * PLANE] = sums_ref[at : at + 1, :]


SMEM = pl.BlockSpec(memory_space=pltpu.SMEM)
VMEM = pl.BlockSpec(memory_space=pltpu.VMEM)
ANY = pl.BlockSpec(memory_space=pl.ANY)


def shards(
    coefficients,
    potential,
    to_values,
    x_kernels,
    yz_kernels,
    two_scale,
    disp_ids,
    dest_box,
    parent_of,
    child_octant,
):
    xk = x_kernels.transpose(0, 2, 1).reshape(TERMS * K, 3 * K)
    octant = child_octant.reshape(1, BOXES)
    ints = functools.partial(jax.ShapeDtypeStruct, dtype=I32)
    slots, labels = pl.pallas_call(
        route_kernel,
        out_shape=(ints((1, TABLE)), ints((DEVICES, 1, PLANE))),
        in_specs=[VMEM] * 3,
        out_specs=(VMEM, VMEM),
    )(dest_box, disp_ids, parent_of.reshape(1, BOXES))
    mat = (ROWS, ROWS)
    dma = pltpu.SemaphoreType.DMA
    shape = jax.ShapeDtypeStruct
    parts = pl.pallas_call(
        main_kernel,
        out_shape=(
            shape(mat, F32),
            shape((BOXES, K, PLANE), BF16),
            shape((2 * K, PLANE), F32),
            shape((4, *mat), BF16),
            shape((3, *mat), BF16),
        ),
        in_specs=[SMEM] + [VMEM] * 7 + [ANY],
        out_specs=(VMEM,) * 5,
        scratch_shapes=[
            pltpu.VMEM((TERMS, PLANE, WIDE), BF16),
            pltpu.VMEM((SHIFTS * BOXES, TERMS * K, PLANE), BF16),
            pltpu.VMEM((HALVES, DEVICES, CAP, K, HALF), BF16),
            pltpu.VMEM((ITERS, HALVES, DEVICES, CAP, K, HALF), BF16),
            pltpu.VMEM((GROUP, K, PLANE), BF16),
            pltpu.VMEM((ITERS, GROUP, K, PLANE), BF16),
            pltpu.VMEM((GROUP, K, PLANE), BF16),
            pltpu.VMEM((ITERS, GROUP, K, PLANE), BF16),
            pltpu.VMEM((DEVICES, 1, PLANE), I32),
            pltpu.VMEM((8, *mat), BF16),
            pltpu.VMEM((4, *mat), BF16),
            pltpu.VMEM((BOXES, K, PLANE), BF16),
            pltpu.VMEM((3, K, TERMS * K), BF16),
            dma((TERMS,)),
            dma((2,)),
            dma((ITERS,)),
            dma((ITERS, HALVES, BURSTS)),
            dma((ITERS, 4)),
        ],
        compiler_params=pltpu.CompilerParams(
            vmem_limit_bytes=VMEM_LIMIT, collective_id=0, has_side_effects=True
        ),
    )(slots, labels, coefficients, potential, to_values, two_scale, octant, xk, yz_kernels)
    return pl.pallas_call(
        last_kernel,
        out_shape=(shape((BOXES, K * PLANE), F32), shape((2, K * PLANE), F32)),
        in_specs=[VMEM] * 6,
        out_specs=(VMEM, VMEM),
    )(*parts, octant)


def solution(mesh):
    spread = P(("oct", "sub"), None)
    placed = (spread, spread, P(), P(), P(), P(), spread, spread, P(("oct", "sub")), P(("oct", "sub")))
    return jax.shard_map(
        shards, mesh=mesh, in_specs=placed, out_specs=(spread, spread), check_vma=False
    )
```

```python
import functools

import jax
import jax.numpy as jnp
from jax import lax
from jax.experimental import pallas as pl
from jax.experimental.pallas import tpu as pltpu
from jax.sharding import PartitionSpec as P

F32, BF16, I32 = jnp.float32, jnp.bfloat16, jnp.int32
MESH = pl.DeviceIdType.MESH
ITERS = 2
K = 16
PLANE = K * K
BOXES = 16
ROWS = BOXES * K
TERMS = 20
SHIFTS = 9
LIST = 16
DEVICES = 128
GROUP = 64
CAP = 2
HALVES, HALF = 2, PLANE // 2
SLOTS = DEVICES * CAP
WIDE = SHIFTS * PLANE
SIDE = 4
BURSTS = GROUP // SIDE
BATCH = DEVICES // BURSTS
UP_BATCH = 16
NO_PARENT = 2
CHILD, HOME, TABLE = 2 * SLOTS, 2 * SLOTS + DEVICES, 2 * SLOTS + 2 * DEVICES
VMEM_LIMIT = 67_000_000


def mm(a, b):
    return jnp.dot(a, b, preferred_element_type=F32)


def split(a):
    hi = a.astype(BF16)
    return hi, (a - hi.astype(F32)).astype(BF16)


def mm3(a, b):
    return mm(a[0], b[0]) + (mm(a[0], b[1]) + mm(a[1], b[0]))


def exact(a, b):
    return jnp.dot(a, b, precision=lax.Precision.HIGHEST, preferred_element_type=F32)


def iotas(shape):
    return lax.broadcasted_iota(I32, shape, 0), lax.broadcasted_iota(I32, shape, 1)


def spreads():
    row, col = iotas((ROWS, K))
    high, low = (row // K == col).astype(F32), (row % K == col).astype(F32)
    row, col = iotas((K, ROWS))
    high_t, low_t = (col // K == row).astype(F32), (col % K == row).astype(F32)
    return high, low, high_t, low_t


def fill_values(table, mats):
    high, low, high_t, low_t = spreads()
    row, col = iotas((ROWS, ROWS))
    table_t = table.T
    hh = exact(exact(high, table), high_t)
    ll = exact(exact(low, table), low_t)
    hh_t = exact(exact(high, table_t), high_t)
    ll_t = exact(exact(low, table_t), low_t)
    lh_t = exact(exact(low, table_t), high_t)
    left = jnp.where(row % K == col % K, hh, 0.0)
    left_back = jnp.where(row // K == col % K, lh_t, 0.0)
    for n, mat in enumerate((left, hh_t * ll_t, left_back, hh * ll)):
        hi, lo = split(mat)
        mats[2 * n] = hi
        mats[2 * n + 1] = lo


def octant_rows(octant_ref, digit):
    row, col = iotas((ROWS, BOXES))
    hit = (row // K if digit == "high" else row % K) == col
    return jnp.sum(jnp.where(hit, octant_ref[...], 0), axis=1, keepdims=True)


def fill_tree(scale_ref, octant_ref, up_mats, down_mats, sides):
    high, low, high_t, low_t = spreads()
    row, col = iotas((ROWS, ROWS))
    filters = [scale_ref[c] for c in range(2)]
    turned = [f.T for f in filters]
    for mats, pair in ((up_mats, turned), (down_mats, filters)):
        highs = [exact(exact(high, f), high_t) for f in pair]
        lows = [exact(exact(low, f), low_t) for f in pair]
        for c in range(4):
            mats[c] = (highs[c // 2] * lows[c % 2]).astype(BF16)
    ups = [exact(exact(low, f), low_t) for f in filters]
    up = jnp.where(octant_rows(octant_ref, "high") // 4 == 1, ups[1], ups[0])
    sides[0] = jnp.where(row // K == col // K, up, 0.0).astype(BF16)
    downs = [exact(exact(high, f), low_t) for f in turned]
    down = jnp.where(octant_rows(octant_ref, "low") // 4 == 1, downs[1], downs[0])
    same = row % K == col // K
    sides[1] = jnp.where(same, down, 0.0).astype(BF16)
    sides[2] = jnp.where(same & (row // K == col % K), 1.0, 0.0).astype(BF16)


def by_octant(blocks, octants, mats):
    out = mm(blocks, mats[0])
    for c in range(1, 4):
        out = jnp.where(octants == c, mm(blocks, mats[c]), out)
    return out


def source_of(current, pot_ref, mats):
    pairs = [(mats[2 * n], mats[2 * n + 1]) for n in range(4)]
    values = mm3(pairs[0], split(mm3(split(current), pairs[1])))
    product = values * (rows_of(pot_ref) + 0.25 * values * values)
    return mm3(pairs[2], split(mm3(split(product), pairs[3]))).astype(BF16)


def corrected(gathered, matched, octants, down_mats, sides):
    inner = by_octant(matched[...].reshape(ROWS, PLANE), octants, down_mats)
    g_hi, g_lo = split(gathered)
    return mm(sides[2], g_hi) + mm(sides[2], g_lo) - mm(sides[1], inner.astype(BF16))


def rows_of(ref):
    return jnp.concatenate([ref[:, x * PLANE : (x + 1) * PLANE] for x in range(K)], axis=0)


def place():
    sub = lax.axis_index("sub")
    return lax.axis_index("oct"), sub // (SIDE * SIDE), (sub // SIDE) % SIDE, sub % SIDE


def burst_of(n, sign):
    core, x, z, y = place()
    a, kz = n // SIDE, lax.rem(n, SIDE)
    z_part = lax.rem(z + sign * kz + SIDE, SIDE) * SIDE
    chips = []
    for ky in range(SIDE):
        x_part = lax.rem(x + sign * (a + kz + ky) + 3 * SIDE, SIDE) * (SIDE * SIDE)
        chips.append(x_part + z_part + lax.rem(y + sign * ky + SIDE, SIDE))
    cores = (core, 1 - core)
    return [[(cores[c], chips[t]) for c in range(2)] for t in range(SIDE)]


def in_bursts(ship, fill=None):
    if fill is None:
        ship(0, 1)

        def step(n, carry):
            ship(n, 0)
            return carry

        lax.fori_loop(1, BURSTS, step, 0)
        return
    fill(0)
    ship(0, 1)
    fill(1)

    def step(n, carry):
        ship(n - 1, 0)
        fill(n)
        return carry

    lax.fori_loop(2, BURSTS, step, 0)
    ship(BURSTS - 1, 0)


def displacement_order(own, core, sub):
    core_0, x, z, y = own
    kx, kz, ky = (sub // 16 - x) & 3, (sub // SIDE - z) & 3, (sub - y) & 3
    u = (((kx - kz - ky) & 3) * SIDE + kz) * SIDE + ky
    return 2 * u + ((core - core_0) & 1)


def whole(a):
    return (a + 1.5).astype(I32) - 1


def route_kernel(dest_ref, disp_ref, parent_ref, table_ref, labels_ref):
    own = place()
    high, low, high_t, low_t = spreads()
    count = BOXES * LIST

    def as_row(v):
        spread = exact(v.astype(F32), low_t)
        return whole(jnp.sum(jnp.where(high_t > 0.5, spread, 0.0), axis=0, keepdims=True))

    def as_col(v):
        spread = exact(high, v.astype(F32))
        return whole(jnp.sum(jnp.where(low > 0.5, spread, 0.0), axis=1, keepdims=True))

    row, col = iotas((count, count))

    def order_of(dest):
        block = dest >> 4
        order = displacement_order(own, block >> 6, block & (GROUP - 1))
        return jnp.where(dest >= 0, order, -1)

    dest_row, dest_col, disp_col = as_row(dest_ref[...]), as_col(dest_ref[...]), as_col(disp_ref[...])
    order_row, order_col = order_of(dest_row), order_of(dest_col)
    same = order_row == order_col
    rank_row = jnp.sum(jnp.where(same & (row < col), 1, 0), axis=0, keepdims=True)
    rank_col = jnp.sum(jnp.where(same & (col < row), 1, 0), axis=1, keepdims=True)
    at_row = jnp.where(order_row >= 0, order_row * CAP + rank_row, -1)
    at_col = jnp.where(order_col >= 0, order_col * CAP + rank_col, -1)
    along_x = (disp_col * 57) >> 9
    box_col = lax.broadcasted_iota(I32, (count, 1), 0) // LIST
    plane_col = (disp_col - SHIFTS * along_x) * BOXES + box_col
    hit = at_col == col
    table_ref[:, :SLOTS] = jnp.sum(jnp.where(hit, plane_col, 0), axis=0, keepdims=True)
    table_ref[:, SLOTS : 2 * SLOTS] = jnp.sum(jnp.where(hit, along_x, 0), axis=0, keepdims=True)

    parent_row = parent_ref[...] & (2 * GROUP - 1)
    up_row = displacement_order(own, own[0], parent_row >> 1)
    row_b, col_b = iotas((BOXES, BOXES))
    up_col = jnp.sum(jnp.where(row_b == col_b, up_row, 0), axis=1, keepdims=True)
    row_u, col_u = iotas((BOXES, DEVICES))
    children = jnp.sum(jnp.where(up_col == 2 * col_u, row_u, 0), axis=0, keepdims=True)
    table_ref[:, CHILD:HOME] = children
    table_ref[:, HOME : HOME + BOXES] = up_row >> 1

    order, lane = iotas((DEVICES, count))
    which = (dest_row & (BOXES - 1)) - BOXES
    labels = [
        jnp.sum(jnp.where(at_row == order * CAP + c, which, 0), axis=1, keepdims=True) + BOXES
        for c in range(CAP)
    ]
    order_b, lane_b = iotas((DEVICES, BOXES))
    ups = jnp.sum(
        jnp.where(up_row == order_b, (parent_row & 1) - NO_PARENT, 0), axis=1, keepdims=True
    )
    marks = jnp.where((lane // K) % CAP == 0, labels[0], labels[1]) + 32 * (ups + NO_PARENT)
    labels_ref[...] = marks.reshape(DEVICES, 1, PLANE)


def main_kernel(
    slots_ref, labels_ref, coef_ref, pot_ref, table_ref, scale_ref, octant_ref, xk_ref, yz_hbm,
    gathered_ref, matched, sums_ref, down_mats, sides,
    yz_buf, partial, send, recv, up_send, up_recv, down_send, down_recv, tags,
    mats, up_mats, lifted, xk,
    yz_sem, tag_sem, send_sem, recv_sem, tree_sem,
):
    for m in range(TERMS):
        pltpu.make_async_copy(
            yz_hbm.at[:, m * WIDE : (m + 1) * WIDE], yz_buf.at[m], yz_sem.at[m]
        ).start()
    barrier = pltpu.get_barrier_semaphore()
    someone = burst_of(jnp.int32(0), 1)[1][0]

    def greet(n, skip):
        devices = burst_of(jnp.int32(n), 1)
        for e in range(skip, BATCH):
            pl.semaphore_signal(
                barrier, inc=1, device_id=devices[e // 2][e % 2], device_id_type=MESH
            )

    in_bursts(greet)

    def remote(source, target, out_sem, in_sem, device):
        return pltpu.make_async_remote_copy(
            src_ref=source, dst_ref=target, send_sem=out_sem, recv_sem=in_sem,
            device_id=device, device_id_type=MESH,
        )

    def arrived(region, out_sem, in_sem):
        remote(region, region, out_sem, in_sem, someone).wait_recv()

    def left(region, out_sem, in_sem):
        remote(region, region, out_sem, in_sem, someone).wait_send()

    xk[...] = xk_ref[...].astype(F32).T.astype(BF16).reshape(3, K, TERMS * K)
    fill_values(table_ref[...], mats)
    source = source_of(rows_of(coef_ref), pot_ref, mats)
    octants = octant_rows(octant_ref, "high") % 4
    row, col = iotas((ROWS, ROWS))
    same_plane = row % K == col % K
    row_box = row // K

    pl.semaphore_wait(barrier, DEVICES - 1)

    def tell(n, skip):
        devices = burst_of(jnp.int32(n), 1)
        for e in range(skip, BATCH):
            j = n * BATCH + e
            remote(
                labels_ref.at[j], tags.at[j], tag_sem.at[0], tag_sem.at[1], devices[e // 2][e % 2]
            ).start()

    tell(0, 1)
    tags[0] = labels_ref[0]

    for it in range(ITERS):

        if it > 0:
            left(send.at[:, pl.ds(1, DEVICES - 1)], send_sem.at[it - 1], recv_sem.at[0, 0, 0])
        for h in range(HALVES):
            lanes = slice(h * HALF, (h + 1) * HALF)

            def product(pair, it=it, source=source, h=h, lanes=lanes):
                if it == 0 and h == 0:
                    for e in range(2):
                        m = 2 * pair + e
                        pltpu.make_async_copy(
                            yz_hbm.at[:, pl.ds(0, WIDE)], yz_buf.at[m], yz_sem.at[m]
                        ).wait()
                at = pl.multiple_of(pair * 2 * K, 2 * K)
                for p in range(SHIFTS):
                    lo = p * PLANE + h * HALF
                    both = jnp.concatenate(
                        [yz_buf[2 * pair + e, :, lo : lo + HALF] for e in range(2)], axis=1
                    )
                    part = mm(source, both).astype(BF16)
                    for e in range(2):
                        partial[p * BOXES : (p + 1) * BOXES, pl.ds(at + e * K, K), lanes] = part[
                            :, e * HALF : (e + 1) * HALF
                        ].reshape(BOXES, K, HALF)

            def step(pair, carry, product=product):
                product(pair)
                return carry

            def telling(pair, carry, product=product):
                for e in range(3):
                    tell(1 + 3 * pair + e, 0)
                product(pair)
                return carry

            if it == 0 and h == 0:
                lax.fori_loop(0, BURSTS // 3, telling, 0)
                lax.fori_loop(BURSTS // 3, TERMS // 2, step, 0)
            else:
                lax.fori_loop(0, TERMS // 2, step, 0, unroll=2)

            def ship(n, skip, it=it, h=h):
                devices = burst_of(jnp.int32(n), 1)
                for e in range(skip, BATCH):
                    j = n * BATCH + e
                    remote(
                        send.at[h, j], recv.at[it, h, j], send_sem.at[it], recv_sem.at[it, h, n],
                        devices[e // 2][e % 2],
                    ).start()

            def fill(n, h=h, lanes=lanes):
                for e in range(BATCH):
                    j = n * BATCH + e
                    at = [j * CAP + c for c in range(CAP)]
                    factors = jnp.concatenate([xk[slots_ref[0, SLOTS + i]] for i in at], axis=0)
                    parts = jnp.concatenate([partial[slots_ref[0, i], :, lanes] for i in at], axis=1)
                    both = mm(factors, parts).astype(BF16)
                    for c in range(CAP):
                        send[h, j, c] = both[c * K : (c + 1) * K, c * HALF : (c + 1) * HALF]

            in_bursts(ship, fill)
            recv[it, h, 0] = send[h, 0]

        if it == 0:
            fill_tree(scale_ref, octant_ref, up_mats, down_mats, sides)
        if it == 0:
            arrived(tags.at[pl.ds(1, DEVICES - 1)], tag_sem.at[0], tag_sem.at[1])

        halves = []
        for h in range(HALVES):
            total = jnp.zeros((ROWS, HALF), F32)
            for g in range(BURSTS):
                lo = max(1, g * BATCH)
                arrived(
                    recv.at[it, h, pl.ds(lo, (g + 1) * BATCH - lo)],
                    send_sem.at[it], recv_sem.at[it, h, g],
                )
                marks = tags[g * BATCH : (g + 1) * BATCH].reshape(BATCH, PLANE) % 32
                row8, col8 = iotas((BATCH, PLANE))
                marks = jnp.sum(
                    jnp.where(row8 == col8 // (CAP * K), marks, 0), axis=0, keepdims=True
                )
                member = jnp.where(same_plane & (marks == row_box), 1.0, 0.0).astype(BF16)
                block = recv[it, h, g * BATCH : (g + 1) * BATCH].reshape(ROWS, HALF)
                total = total + mm(member, block)
            halves.append(total)
        gathered = jnp.concatenate(halves, axis=1)

        inner = by_octant(gathered.astype(BF16), octants, up_mats)
        up = mm(sides[0], inner.astype(BF16))
        lifted[...] = up.astype(BF16).reshape(BOXES, K, PLANE)

        if it > 0:
            left(up_send.at[pl.ds(1, GROUP - 1)], tree_sem.at[it - 1, 0], tree_sem.at[0, 1])

        def ship_up(n, skip, it=it):
            devices = burst_of(jnp.int32(n), 1)
            for t in range(skip, SIDE):
                u = n * SIDE + t
                remote(
                    up_send.at[u], up_recv.at[it, u], tree_sem.at[it, 0], tree_sem.at[it, 1],
                    devices[t][0],
                ).start()

        def fill_up(n):
            for t in range(SIDE):
                up_send[n * SIDE + t] = lifted[slots_ref[0, CHILD + n * SIDE + t]]

        in_bursts(ship_up, fill_up)
        up_recv[it, 0] = up_send[0]
        arrived(up_recv.at[it, pl.ds(1, GROUP - 1)], tree_sem.at[it, 0], tree_sem.at[it, 1])

        sums = jnp.zeros((2 * K, PLANE), F32)
        row_p, col_p = iotas((2 * K, PLANE))
        for h in range(GROUP // UP_BATCH):
            span = 2 * UP_BATCH
            marks = tags[h * span : (h + 1) * span].reshape(span, PLANE) // 32
            row_s, col_s = iotas((span, PLANE))
            marks = jnp.sum(jnp.where(row_s == 2 * (col_s // K), marks, 0), axis=0, keepdims=True)
            member = jnp.where((row_p % K == col_p % K) & (marks == row_p // K), 1.0, 0.0)
            block = up_recv[it, h * UP_BATCH : (h + 1) * UP_BATCH].reshape(ROWS, PLANE)
            sums = sums + mm(member.astype(BF16), block)
        if it == ITERS - 1:
            sums_ref[...] = sums
            gathered_ref[...] = gathered

        if it > 0:
            left(down_send.at[pl.ds(1, GROUP - 1)], tree_sem.at[it - 1, 2], tree_sem.at[0, 3])

        def ship_down(n, skip, it=it):
            devices = burst_of(jnp.int32(n), -1)
            for t in range(skip, SIDE):
                u = n * SIDE + t
                remote(
                    down_send.at[u], down_recv.at[it, u], tree_sem.at[it, 2], tree_sem.at[it, 3],
                    devices[t][0],
                ).start()

        def fill_down(n, sums=sums):
            for t in range(SIDE):
                second = tags[2 * (n * SIDE + t)] // 32 == 1
                down_send[n * SIDE + t] = jnp.where(second, sums[K:], sums[:K]).astype(BF16)

        in_bursts(ship_down, fill_down)
        down_recv[it, 0] = down_send[0]
        arrived(down_recv.at[it, pl.ds(1, GROUP - 1)], tree_sem.at[it, 2], tree_sem.at[it, 3])

        for b in range(BOXES):
            matched[b] = down_recv[it, slots_ref[0, HOME + b]]
        if it < ITERS - 1:
            current = corrected(gathered, matched, octants, down_mats, sides)
            source = source_of(current, pot_ref, mats)

    last = ITERS - 1
    left(tags.at[pl.ds(1, DEVICES - 1)], tag_sem.at[0], tag_sem.at[1])
    left(send.at[:, pl.ds(1, DEVICES - 1)], send_sem.at[last], recv_sem.at[0, 0, 0])
    left(up_send.at[pl.ds(1, GROUP - 1)], tree_sem.at[last, 0], tree_sem.at[0, 1])
    left(down_send.at[pl.ds(1, GROUP - 1)], tree_sem.at[last, 2], tree_sem.at[0, 3])


def last_kernel(gathered_ref, matched, sums_ref, down_mats, sides, octant_ref, field_ref, parents_ref):
    octants = octant_rows(octant_ref, "high") % 4
    current = corrected(gathered_ref[...], matched, octants, down_mats, sides)
    for x in range(K):
        field_ref[:, x * PLANE : (x + 1) * PLANE] = current[x * BOXES : (x + 1) * BOXES, :]
    for p in range(2):
        for i in range(K):
            at = p * K + i
            parents_ref[p : p + 1, i * PLANE : (i + 1) * PLANE] = sums_ref[at : at + 1, :]


SMEM = pl.BlockSpec(memory_space=pltpu.SMEM)
VMEM = pl.BlockSpec(memory_space=pltpu.VMEM)
ANY = pl.BlockSpec(memory_space=pl.ANY)


def shards(
    coefficients,
    potential,
    to_values,
    x_kernels,
    yz_kernels,
    two_scale,
    disp_ids,
    dest_box,
    parent_of,
    child_octant,
):
    xk = x_kernels.transpose(0, 2, 1).reshape(TERMS * K, 3 * K)
    octant = child_octant.reshape(1, BOXES)
    ints = functools.partial(jax.ShapeDtypeStruct, dtype=I32)
    slots, labels = pl.pallas_call(
        route_kernel,
        out_shape=(ints((1, TABLE)), ints((DEVICES, 1, PLANE))),
        in_specs=[VMEM] * 3,
        out_specs=(VMEM, VMEM),
    )(dest_box, disp_ids, parent_of.reshape(1, BOXES))
    mat = (ROWS, ROWS)
    dma = pltpu.SemaphoreType.DMA
    shape = jax.ShapeDtypeStruct
    parts = pl.pallas_call(
        main_kernel,
        out_shape=(
            shape(mat, F32),
            shape((BOXES, K, PLANE), BF16),
            shape((2 * K, PLANE), F32),
            shape((4, *mat), BF16),
            shape((3, *mat), BF16),
        ),
        in_specs=[SMEM] + [VMEM] * 7 + [ANY],
        out_specs=(VMEM,) * 5,
        scratch_shapes=[
            pltpu.VMEM((TERMS, PLANE, WIDE), BF16),
            pltpu.VMEM((SHIFTS * BOXES, TERMS * K, PLANE), BF16),
            pltpu.VMEM((HALVES, DEVICES, CAP, K, HALF), BF16),
            pltpu.VMEM((ITERS, HALVES, DEVICES, CAP, K, HALF), BF16),
            pltpu.VMEM((GROUP, K, PLANE), BF16),
            pltpu.VMEM((ITERS, GROUP, K, PLANE), BF16),
            pltpu.VMEM((GROUP, K, PLANE), BF16),
            pltpu.VMEM((ITERS, GROUP, K, PLANE), BF16),
            pltpu.VMEM((DEVICES, 1, PLANE), I32),
            pltpu.VMEM((8, *mat), BF16),
            pltpu.VMEM((4, *mat), BF16),
            pltpu.VMEM((BOXES, K, PLANE), BF16),
            pltpu.VMEM((3, K, TERMS * K), BF16),
            dma((TERMS,)),
            dma((2,)),
            dma((ITERS,)),
            dma((ITERS, HALVES, BURSTS)),
            dma((ITERS, 4)),
        ],
        compiler_params=pltpu.CompilerParams(
            vmem_limit_bytes=VMEM_LIMIT, collective_id=0, has_side_effects=True
        ),
    )(slots, labels, coefficients, potential, to_values, two_scale, octant, xk, yz_kernels)
    return pl.pallas_call(
        last_kernel,
        out_shape=(shape((BOXES, K * PLANE), F32), shape((2, K * PLANE), F32)),
        in_specs=[VMEM] * 6,
        out_specs=(VMEM, VMEM),
    )(*parts, octant)


def solution(mesh):
    spread = P(("oct", "sub"), None)
    placed = (spread, spread, P(), P(), P(), P(), spread, spread, P(("oct", "sub")), P(("oct", "sub")))
    return jax.shard_map(
        shards, mesh=mesh, in_specs=placed, out_specs=(spread, spread), check_vma=False
    )
```
